32 devices in a mesh: ctx: 4 (over y, x), head: 8 (over z, core).
Axes of the slice: x: 2, y: 2, z: 4, core: 2. Of those that a mesh axis runs over, the one named last changes fastest.
Arguments:
- query_rows: bfloat16 [4096, 8192], P('ctx', 'head'), may hold values from -6 to 6
- key_rows: bfloat16 [4096, 8192], P('ctx', 'head'), may hold values from -6 to 6
- value_rows: bfloat16 [4096, 8192], P('ctx', 'head'), may hold values from -6 to 6
- decay_rate: float32 [64], P('head'), as said below
- starts: int32 [4096], P('ctx'), may hold values 0 or 1
- norm_gain: float32 [8192], P('head'), may hold values from 0.1 to 1.9
- grad_out: bfloat16 [4096, 8192], P('ctx', 'head'), may hold values from -6 to 6
Outputs:
- normed: bfloat16 [4096, 8192], P('ctx', 'head')
- grad_query: bfloat16 [4096, 8192], P('ctx', 'head')
- grad_key: bfloat16 [4096, 8192], P('ctx', 'head')
- grad_value: bfloat16 [4096, 8192], P('ctx', 'head')
The draws below stay inside these ranges and needn't reach their ends.
Inputs may be any that keep to these rules, and one draw needn't show every extreme that they name: `decay_rate`: positive rates; a head keeps exp(-rate) of its state per position. `starts`: 1 where a document begins, 0 elsewhere.
All inputs are finite; a program needn't handle non-finite values. No bound on the sum of `starts` on one device may be relied on, other than what follows from the above.
Results may differ from the reference program's by a relative error of at most 0.008.
Values sent between devices are 32-bit elements; how exact they have to be, the bound alone decides.
A program may use at most 128 MiB of HBM per device.

```python
import math
import jax
import jax.numpy as jnp
from jax import lax

HEADS = 64
DH = 128
TOK_DEV = 1024
BLOCK = 512
TOKENS = 4096


def draw_decay_rate(key, part):
    pick_key, fast_key, slow_key = jax.random.split(key, 3)
    share = 0.5
    chosen = jax.random.uniform(pick_key, (HEADS,)) < share
    fast = jnp.exp(jax.random.uniform(fast_key, (HEADS,), minval=math.log(1.0 / 50.0), maxval=math.log(1.0 / 15.0)))
    slow = jnp.exp(jax.random.uniform(slow_key, (HEADS,), minval=math.log(0.2 / TOKENS), maxval=math.log(2.2 / TOKENS)))
    return jnp.where(chosen, fast, slow).astype(jnp.float32)


def touch_ends(drawn, stream_key, least, top_value):
    longest = drawn.shape.index(max(drawn.shape))
    spots = []
    for shift in (0, 1):
        where = [jax.random.randint(jax.random.fold_in(stream_key, axis), (), 0, length) for axis, length in enumerate(drawn.shape)]
        where[longest] = (where[longest] + shift) % drawn.shape[longest]
        spots.append(tuple(where))
    return drawn.at[spots[0]].set(least).at[spots[1]].set(top_value)


def shard_levels(stream_key, dims, shards, least, high):
    factor_of, own = 1.0, jax.random.fold_in(stream_key, 6)
    for dim, blocks in shards:
        heights = jnp.exp(jax.random.uniform(jax.random.fold_in(own, dim), (blocks,), jnp.float32, least / len(shards), high / len(shards)))
        factor_of = factor_of * jnp.repeat(heights, dims[dim] // blocks).reshape([-1 if axis == dim else 1 for axis in range(len(dims))])
    return factor_of


def normal_values(key, shape, scale, most, cuts=(), dtype=jnp.bfloat16):
    result = scale * jax.random.normal(key, shape, jnp.float32)
    if cuts:
        result = result * shard_levels(key, shape, cuts, -0.22, 0.18)
    return jnp.clip(result, -most, most).astype(dtype)


def setup_inputs(seed: int = 0) -> dict:
    streams_of = jax.random.split(jax.random.key(seed), 8)
    query_rows = normal_values(streams_of[0], (TOKENS, HEADS * DH), 1.0, 6.0, ((0, 4), (1, 8)))
    key_rows = normal_values(streams_of[1], (TOKENS, HEADS * DH), 1.0, 6.0, ((0, 4), (1, 8)))
    value_rows = normal_values(streams_of[2], (TOKENS, HEADS * DH), 1.0, 6.0, ((0, 4), (1, 8)))
    decay_rate = draw_decay_rate(jax.random.fold_in(streams_of[7], 71), 0)
    starts = touch_ends((jax.random.randint(streams_of[4], (TOKENS,), 0, 8 * TOK_DEV) < 1).astype(jnp.int32), jax.random.fold_in(streams_of[4], 1), 0, 1)
    norm_gain = jnp.clip(1.0 + 0.18 * jax.random.normal(streams_of[5], (HEADS * DH,), jnp.float32), 0.1, 1.9)
    grad_out = normal_values(streams_of[6], (TOKENS, HEADS * DH), 1.0, 6.0, ((0, 4), (1, 8)))
    return dict(query_rows=query_rows, key_rows=key_rows, value_rows=value_rows, decay_rate=decay_rate, starts=starts, norm_gain=norm_gain, grad_out=grad_out)


HIGH = lax.Precision.HIGHEST
EPSILON = 1e-06

def block_masks(flags, rates, width):
    running = jnp.cumsum(flags).astype(jnp.int32)
    place = jnp.arange(width).astype(jnp.float32)
    offset = place[:, None] - place[None, :]
    joined = (running[:, None] == running[None, :]) & (offset >= 0.0)
    decay_mask = jnp.where(joined[None], jnp.exp(-rates[:, None, None] * jnp.maximum(offset, 0.0)[None]), 0.0)
    reach_in = jnp.where((running == 0)[None], jnp.exp(-rates[:, None] * (place + 1.0)[None]), 0.0)
    reach_out = jnp.where((running == running[-1])[None], jnp.exp(-rates[:, None] * (width - 1.0 - place)[None]), 0.0)
    carry_over = jnp.where(running[-1] == 0, jnp.exp(-rates * width), 0.0)
    return (decay_mask, reach_in, reach_out, carry_over)

def reference(query_rows, key_rows, value_rows, decay_rate, starts, norm_gain, grad_out):
    blocks = TOKENS // BLOCK
    layout = (blocks, BLOCK, HEADS, DH)
    query_blocks = query_rows.reshape(layout)
    key_blocks = key_rows.reshape(layout)
    value_blocks = value_rows.reshape(layout)
    flag_blocks = starts.reshape(blocks, BLOCK)

    def forward_step(state, inputs):
        query_block, key_block, value_block, flags = inputs
        decay_mask, reach_in, reach_out, carry_over = block_masks(flags, decay_rate, BLOCK)
        query_wide = query_block.astype(jnp.float32)
        key_wide = key_block.astype(jnp.float32)
        value_wide = value_block.astype(jnp.float32)
        scores = jnp.einsum('thd,shd->hts', query_wide, key_wide, precision=HIGH)
        weights = lax.optimization_barrier((scores * decay_mask).astype(jnp.bfloat16)).astype(jnp.float32)
        local_out = jnp.einsum('hts,she->the', weights, value_wide, precision=HIGH)
        carried = jnp.transpose(reach_in)[:, :, None] * jnp.einsum('thd,hde->the', query_wide, state, precision=HIGH)
        weighted_keys = key_wide * jnp.transpose(reach_out)[:, :, None]
        new_state = carry_over[:, None, None] * state + jnp.einsum('shd,she->hde', weighted_keys, value_wide, precision=HIGH)
        return (new_state, (local_out + carried, state))
    zero_state = jnp.zeros((HEADS, DH, DH), jnp.float32)
    last_state, (attended, before) = lax.scan(forward_step, zero_state, (query_blocks, key_blocks, value_blocks, flag_blocks))
    outputs = attended.reshape(TOKENS, HEADS * DH)
    inverse = 1.0 / jnp.sqrt(lax.optimization_barrier(jnp.mean(outputs * outputs, axis=1)) + EPSILON)
    normed = (outputs * inverse[:, None] * norm_gain[None, :]).astype(jnp.bfloat16)
    gained = grad_out.astype(jnp.float32) * norm_gain[None, :]
    cross = lax.optimization_barrier(jnp.mean(gained * outputs, axis=1))
    grad_att = (inverse[:, None] * gained - outputs * (inverse * inverse * inverse * cross)[:, None]).astype(jnp.bfloat16)
    grad_blocks = grad_att.reshape(layout)

    def backward_step(later, inputs):
        query_block, key_block, value_block, flags, grad_block, state = inputs
        decay_mask, reach_in, reach_out, carry_over = block_masks(flags, decay_rate, BLOCK)
        query_wide = query_block.astype(jnp.float32)
        key_wide = key_block.astype(jnp.float32)
        value_wide = value_block.astype(jnp.float32)
        grad_wide = grad_block.astype(jnp.float32)
        scores = jnp.einsum('thd,shd->hts', query_wide, key_wide, precision=HIGH)
        weights = lax.optimization_barrier((scores * decay_mask).astype(jnp.bfloat16)).astype(jnp.float32)
        grad_weights = jnp.einsum('the,she->hts', grad_wide, value_wide, precision=HIGH)
        grad_scores = lax.optimization_barrier((grad_weights * decay_mask).astype(jnp.bfloat16)).astype(jnp.float32)
        grad_query = jnp.einsum('hts,shd->thd', grad_scores, key_wide, precision=HIGH)
        grad_query = grad_query + jnp.transpose(reach_in)[:, :, None] * jnp.einsum('the,hde->thd', grad_wide, state, precision=HIGH)
        grad_key = jnp.einsum('hts,thd->shd', grad_scores, query_wide, precision=HIGH)
        grad_key = grad_key + jnp.transpose(reach_out)[:, :, None] * jnp.einsum('she,hde->shd', value_wide, later, precision=HIGH)
        grad_value = jnp.einsum('hts,the->she', weights, grad_wide, precision=HIGH)
        grad_value = grad_value + jnp.transpose(reach_out)[:, :, None] * jnp.einsum('shd,hde->she', key_wide, later, precision=HIGH)
        earlier = carry_over[:, None, None] * later + jnp.einsum('thd,the->hde', query_wide * jnp.transpose(reach_in)[:, :, None], grad_wide, precision=HIGH)
        return (earlier, (grad_query.astype(jnp.bfloat16), grad_key.astype(jnp.bfloat16), grad_value.astype(jnp.bfloat16)))
    first_grad, (grad_query, grad_key, grad_value) = lax.scan(backward_step, zero_state, (query_blocks, key_blocks, value_blocks, flag_blocks, grad_blocks, before), reverse=True)
    shape_out = (TOKENS, HEADS * DH)
    return (normed, grad_query.reshape(shape_out), grad_key.reshape(shape_out), grad_value.reshape(shape_out))
```

```python
import functools

import jax
import jax.numpy as jnp
from jax import lax
from jax.experimental import pallas as pl
from jax.experimental.pallas import tpu as pltpu
from jax.sharding import PartitionSpec as P

HEADS = 64
DH = 128
CHUNK = 128
AHEAD = 2
AHEAD_GRADS = 3
EPSILON = 1e-06
MESH = pl.DeviceIdType.MESH
F32 = jnp.float32
BF16 = jnp.bfloat16


def dot(a, b, da, db):
    return lax.dot_general(a, b, (((da,), (db,)), ((), ())), preferred_element_type=F32)


def kernel(
    shards, steps, peers, total,
    q_hbm, k_hbm, v_hbm, g_hbm, rate_ref, starts_ref, gain_ref,
    n_out, gq_out, gk_out, gv_out,
    qs, ks, vs, gs, att, ga, weights, gkp, gvp,
    joined, in_mask, out_mask, clear, d_state, full_state, d_grad,
    own, got, pre, flags_buf, kept_buf, sq_acc, cr_acc, inv_full, coef_full, x_buf,
    in_sem, s_send, s_recv, f_send, f_recv, x_send, x_recv,
):
    heads, rows, _ = qs.shape
    chunks = rows // CHUNK
    ctx = lax.axis_index("ctx")
    me = lax.axis_index("head")

    def cols(h):
        return pl.ds(pl.multiple_of(h * DH, DH), DH)

    def load(i, h):
        hbm, buf = ((k_hbm, ks), (v_hbm, vs), (q_hbm, qs), (g_hbm, gs))[i]
        return pltpu.make_async_copy(hbm.at[:, cols(h)], buf.at[h], in_sem.at[i, h])

    def size_of(late, step):
        return 1 << (steps - 1 - step if late else step)

    def scan_copy(which, step, h, late):
        size = size_of(late, step)
        return pltpu.make_async_remote_copy(
            src_ref=own.at[which, step, h],
            dst_ref=got.at[which, step, h],
            send_sem=s_send.at[which, step, h],
            recv_sem=s_recv.at[which, step, h],
            device_id=(ctx + size - 2 * size * ((ctx // size) % 2), me),
            device_id_type=MESH,
        )

    def flag_copy(k):
        return pltpu.make_async_remote_copy(
            src_ref=flags_buf.at[ctx],
            dst_ref=flags_buf.at[ctx],
            send_sem=f_send.at[k],
            recv_sem=f_recv.at[k],
            device_id=((ctx + k) % shards, me),
            device_id_type=MESH,
        )

    def swap_copy(k):
        return pltpu.make_async_remote_copy(
            src_ref=x_buf.at[0],
            dst_ref=x_buf.at[k],
            send_sem=x_send.at[k],
            recv_sem=x_recv.at[k],
            device_id=(ctx, (me + k) % peers),
            device_id_type=MESH,
        )

    def start_loads(pair):
        def go(h, c):
            for i in pair:
                load(i, h).start()
            return c
        lax.fori_loop(0, heads, go, 0)

    start_loads((0, 1))
    start_loads((2, 3))

    barrier = pltpu.get_barrier_semaphore()
    for k in range(1, shards):
        pl.semaphore_signal(
            barrier, inc=1, device_id=((ctx + k) % shards, me), device_id_type=MESH
        )

    def greet(k, c):
        pl.semaphore_signal(
            barrier, inc=1, device_id=(ctx, (me + k) % peers), device_id_type=MESH
        )
        return c

    lax.fori_loop(1, peers, greet, 0)

    row_at = lax.broadcasted_iota(jnp.int32, (CHUNK, CHUNK), 0)
    col_at = lax.broadcasted_iota(jnp.int32, (CHUNK, CHUNK), 1)
    lower = row_at >= col_at
    ones_low = jnp.where(lower, 1.0, 0.0).astype(BF16)
    for c in range(chunks):
        flags = starts_ref[:, c * CHUNK:(c + 1) * CHUNK].astype(F32)
        wide = jnp.broadcast_to(flags, (DH, CHUNK)).astype(BF16)
        run_row = dot(wide, ones_low, 1, 1)[0:1, :]
        run_col = dot(ones_low, wide, 1, 1)
        count = jnp.sum(flags, axis=1, keepdims=True)
        both = jnp.concatenate([run_col] * (CHUNK // DH), axis=1)
        joined[c] = jnp.where(lower & (both == run_row), 1.0, 0.0)
        in_mask[c] = jnp.where(run_col == 0.0, 1.0, 0.0)
        out_mask[c] = jnp.where(run_col == count, 1.0, 0.0)
        clear[c] = jnp.broadcast_to(jnp.where(count == 0.0, 1.0, 0.0), (8, DH))
    whole = jnp.sum(starts_ref[...].astype(F32), axis=1, keepdims=True)
    flags_buf[ctx] = jnp.broadcast_to(jnp.where(whole == 0.0, 1.0, 0.0), (8, DH))
    sq_acc[...] = jnp.zeros_like(sq_acc)
    cr_acc[...] = jnp.zeros_like(cr_acc)

    place = lax.broadcasted_iota(jnp.int32, (CHUNK, DH), 0).astype(F32)
    gap = jnp.maximum(row_at - col_at, 0).astype(F32)

    def reach_in(rate):
        return jnp.exp(-rate * (place + 1.0))

    def reach_out(rate):
        return jnp.exp(-rate * (CHUNK - 1.0 - place))

    def carry(rate, c):
        return clear[c] * jnp.exp(jnp.full((8, DH), -rate * CHUNK, F32))

    table = {}

    def factor(which, first, last, use, other):
        kept = jnp.ones((8, DH), F32)
        for i in range(shards):
            flag = flags_buf[shards - 1 - i if which else i]
            kept = kept * jnp.where((i >= first) & (i < last), flag, 1.0)
        slot = sum(len(entry) for entry in table.values())
        kept_buf[slot] = jnp.where(use, kept, other)
        return slot, jnp.where(use, jnp.maximum(last - first, 0) * rows, 0).astype(F32)

    def make_table():
        for which in range(2):
            at = shards - 1 - ctx if which else ctx
            for late in (False, True):
                for step in range(steps):
                    size = size_of(late, step)
                    start = at - at % (2 * size)
                    middle, end, upper = start + size, start + 2 * size, at >= start + size
                    key = (which, late, step)
                    table[key] = []
                    if not late:
                        entries = [(middle, at, upper, 0.0), (middle, end, ~upper, 1.0), (middle, end, upper, 1.0)]
                    else:
                        size = size_of(late, min(step + 1, steps - 1))
                        begin = at - at % (2 * size)
                        half = begin + size
                        lower = at < half
                        first = (at - middle + start + 1, middle, upper, 0.0) if step == 0 else (start, middle, upper, 1.0)
                        entries = [first, (begin, half, lower, 1.0), (at + 1, half, lower, 0.0)]
                    for entry in entries[:1] if step == steps - 1 else entries:
                        table[key] = table[key] + [factor(which, *entry)]

    def put(which, h, late, state):
        own[which, 0, h] = state
        scan_copy(which, 0, h, late).start()

    def take(which, step, h, late, rate):
        scan_copy(which, step, h, late).wait_recv()
        factors = [
            (kept_buf[slot] * jnp.exp(jnp.full((8, DH), -rate * length, F32)))[0:1, :]
            for slot, length in table[which, late, step]
        ]
        came = got[which, step, h]
        if not late:
            state = factors[0] * came
            if step > 0:
                state = state + pre[h]
        else:
            state = factors[0] * (came if step == 0 else pre[h])
            if step > 0:
                state = state + came
        if step == steps - 1:
            return state
        pre[h] = state
        own[which, step + 1, h] = (
            factors[1] * state + factors[2] * own[which, 0, h]
            if late
            else factors[1] * own[which, step, h] + factors[2] * came
        )
        scan_copy(which, step + 1, h, late).start()
        return None

    def pairs(work):
        def go(j, carried):
            for late in (False, True):
                work(2 * j + int(late), late)
            return carried
        lax.fori_loop(0, heads // 2, go, 0)

    def part(c):
        return slice(c * CHUNK, (c + 1) * CHUNK)

    pl.semaphore_wait(barrier, shards + peers - 2)
    for k in range(1, shards):
        flag_copy(k).start()

    def make_states(h, late):
        load(0, h).wait()
        load(1, h).wait()
        rate = rate_ref[h]
        out = reach_out(rate)
        state = jnp.zeros((DH, DH), F32)
        for c in range(chunks):
            weighted = (ks[h, part(c), :].astype(F32) * (out * out_mask[c])).astype(BF16)
            add = dot(weighted, vs[h, part(c), :], 0, 0)
            d_state[h, c] = add
            keep = carry(rate, c)
            state = keep[0:1, :] * state + add
        put(0, h, late, state)

    pairs(make_states)
    for k in range(1, shards):
        flag_copy(k).wait_recv()
    make_table()

    def attend(h):
        load(2, h).wait()
        load(3, h).wait()
        decay = jnp.exp(-rate_ref[h] * gap)
        def raw(c):
            return dot(qs[h, part(c), :], ks[h, part(c), :], 1, 1)

        ready = [raw(c) for c in range(min(AHEAD, chunks))]
        for c in range(chunks):
            scores = ready.pop(0)
            if c + AHEAD < chunks:
                ready.append(raw(c + AHEAD))
            w = (scores * (decay * joined[c])).astype(BF16)
            weights[h, c] = jnp.transpose(w)
            att[h, part(c), :] = dot(w, vs[h, part(c), :], 1, 0)

    def attend_pair(j, carried):
        attend(2 * j)
        attend(2 * j + 1)
        for step in range(steps - 1):
            for late in (False, True):
                h = 2 * j + int(late)
                take(0, step, h, late, rate_ref[h])
        return carried

    lax.fori_loop(0, heads // 2, attend_pair, 0)

    def finish_attend(h, late):
        rate = rate_ref[h]
        state = take(0, steps - 1, h, late, rate)
        reach = reach_in(rate)
        gain = gain_ref[pl.ds(h, 1), :]
        for c in range(chunks):
            small = state.astype(BF16)
            full_state[h, c] = small
            a = att[h, part(c), :] + (reach * in_mask[c]) * dot(qs[h, part(c), :], small, 1, 0)
            att[h, part(c), :] = a
            sq_acc[part(c), :] += a * a
            cr_acc[part(c), :] += gs[h, part(c), :].astype(F32) * gain * a
            if c < chunks - 1:
                state = carry(rate, c)[0:1, :] * state + d_state[h, c]

    pairs(finish_attend)

    x_buf[0, 0:1, :] = jnp.sum(jnp.transpose(sq_acc[...]), axis=0, keepdims=True)
    x_buf[0, 1:2, :] = jnp.sum(jnp.transpose(cr_acc[...]), axis=0, keepdims=True)

    def send(k, c):
        swap_copy(k).start()
        return c

    lax.fori_loop(1, peers, send, 0)

    def receive(k, c):
        swap_copy(k).wait_recv()
        return c + x_buf[k]

    sums = lax.fori_loop(1, peers, receive, x_buf[0])
    inverse = 1.0 / jnp.sqrt(sums[0:1, :] / total + EPSILON)
    coef = inverse * inverse * inverse * (sums[1:2, :] / total)
    inv_full[...] = jnp.transpose(jnp.broadcast_to(inverse, (DH, rows)))
    coef_full[...] = jnp.transpose(jnp.broadcast_to(coef, (DH, rows)))

    def make_grads(h, late):
        rate = rate_ref[h]
        reach = reach_in(rate)
        gain = gain_ref[pl.ds(h, 1), :]
        state = jnp.zeros((DH, DH), F32)
        for c in reversed(range(chunks)):
            a, inv = att[h, part(c), :], inv_full[part(c), :]
            n_out[part(c), cols(h)] = (a * inv * gain).astype(BF16)
            gained = gs[h, part(c), :].astype(F32) * gain
            grad = (inv * gained - a * coef_full[part(c), :]).astype(BF16)
            ga[h, part(c), :] = grad
            weighted = (qs[h, part(c), :].astype(F32) * (reach * in_mask[c])).astype(BF16)
            add = dot(weighted, grad, 0, 0)
            d_grad[h, c] = add
            keep = carry(rate, c)
            state = keep[0:1, :] * state + add
        put(1, h, late, state)

    pairs(make_grads)

    def inner_grads(h):
        rate = rate_ref[h]
        decay = jnp.exp(-rate * gap)
        reach = reach_in(rate)
        def raw(c):
            grad = ga[h, part(c), :]
            return dot(grad, vs[h, part(c), :], 1, 1), dot(grad, full_state[h, c], 1, 1)

        ready = [raw(c) for c in range(min(AHEAD_GRADS, chunks))]
        for c in range(chunks):
            wide, far = ready.pop(0)
            if c + AHEAD_GRADS < chunks:
                ready.append(raw(c + AHEAD_GRADS))
            gvp[h, part(c), :] = dot(weights[h, c], ga[h, part(c), :], 1, 0)
            d = (wide * (decay * joined[c])).astype(BF16)
            gq = dot(d, ks[h, part(c), :], 1, 0) + (reach * in_mask[c]) * far
            gq_out[part(c), cols(h)] = gq.astype(BF16)
            gkp[h, part(c), :] = dot(d, qs[h, part(c), :], 0, 0)

    def inner_pair(j, carried):
        for step in range(steps - 1):
            for late in (False, True):
                h = 2 * j + int(late)
                take(1, step, h, late, rate_ref[h])
        inner_grads(2 * j)
        inner_grads(2 * j + 1)
        return carried

    lax.fori_loop(0, heads // 2, inner_pair, 0)

    def finish_grads(h, late):
        rate = rate_ref[h]
        state = take(1, steps - 1, h, late, rate)
        out = reach_out(rate)
        for c in reversed(range(chunks)):
            small = state.astype(BF16)
            reach = out * out_mask[c]
            gk = gkp[h, part(c), :] + reach * dot(vs[h, part(c), :], small, 1, 1)
            gv = gvp[h, part(c), :] + reach * dot(ks[h, part(c), :], small, 1, 0)
            gk_out[part(c), cols(h)] = gk.astype(BF16)
            gv_out[part(c), cols(h)] = gv.astype(BF16)
            if c > 0:
                state = carry(rate, c)[0:1, :] * state + d_grad[h, c]

    pairs(finish_grads)

    def drain(h, late):
        for which in range(2):
            for step in range(steps):
                scan_copy(which, step, h, late).wait_send()

    pairs(drain)
    for k in range(1, shards):
        flag_copy(k).wait_send()

    def drain_swaps(k, c):
        swap_copy(k).wait_send()
        return c

    lax.fori_loop(1, peers, drain_swaps, 0)


def write_out(*refs):
    sems = refs[8]
    copies = [pltpu.make_async_copy(refs[i], refs[i + 4], sems.at[i]) for i in range(4)]
    for copy in copies:
        copy.start()
    for copy in copies:
        copy.wait()


def body(shards, peers, query_rows, key_rows, value_rows, decay_rate, starts, norm_gain, grad_out):
    rows, features = query_rows.shape
    heads = features // DH
    chunks = rows // CHUNK
    steps = (shards - 1).bit_length()
    big = jax.ShapeDtypeStruct((rows, features), BF16)
    whole = pl.BlockSpec(memory_space=pltpu.HBM)
    inside = pl.BlockSpec(memory_space=pltpu.VMEM)

    def head_rows(dtype):
        return pltpu.VMEM((heads, rows, DH), dtype)

    dma = pltpu.SemaphoreType.DMA
    kept = pl.pallas_call(
        functools.partial(kernel, shards, steps, peers, HEADS * DH),
        out_shape=(pltpu.VMEM((rows, features), BF16),) * 4,
        in_specs=[whole] * 4 + [pl.BlockSpec(memory_space=pltpu.SMEM), inside, inside],
        out_specs=(inside,) * 4,
        scratch_shapes=[head_rows(BF16)] * 4
        + [head_rows(F32), head_rows(BF16), pltpu.VMEM((heads, chunks, CHUNK, CHUNK), BF16)]
        + [head_rows(F32)] * 2
        + [
            pltpu.VMEM((chunks, CHUNK, CHUNK), F32),
            pltpu.VMEM((chunks, CHUNK, DH), F32),
            pltpu.VMEM((chunks, CHUNK, DH), F32),
            pltpu.VMEM((chunks, 8, DH), F32),
            pltpu.VMEM((heads, chunks, DH, DH), F32),
            pltpu.VMEM((heads, chunks, DH, DH), BF16),
            pltpu.VMEM((heads, chunks, DH, DH), F32),
            pltpu.VMEM((2, steps, heads, DH, DH), F32),
            pltpu.VMEM((2, steps, heads, DH, DH), F32),
            pltpu.VMEM((heads, DH, DH), F32),
            pltpu.VMEM((shards, 8, DH), F32),
            pltpu.VMEM((12 * steps, 8, DH), F32),
            pltpu.VMEM((rows, DH), F32),
            pltpu.VMEM((rows, DH), F32),
            pltpu.VMEM((rows, DH), F32),
            pltpu.VMEM((rows, DH), F32),
            pltpu.VMEM((peers, 2, rows), F32),
            dma((4, heads)),
            dma((2, steps, heads)),
            dma((2, steps, heads)),
            dma((shards,)),
            dma((shards,)),
            dma((peers,)),
            dma((peers,)),
        ],
        compiler_params=pltpu.CompilerParams(
            collective_id=0, has_side_effects=True, vmem_limit_bytes=55 * 1024 * 1024
        ),
    )(
        query_rows, key_rows, value_rows, grad_out, decay_rate,
        starts.reshape(1, rows), norm_gain.reshape(heads, DH),
    )
    return pl.pallas_call(
        write_out,
        out_shape=(big,) * 4,
        in_specs=[pl.BlockSpec(memory_space=pl.ANY)] * 4,
        out_specs=(whole,) * 4,
        scratch_shapes=[dma((4,))],
        compiler_params=pltpu.CompilerParams(vmem_limit_bytes=1024 * 1024),
    )(*kept)


def solution(mesh):
    both = P("ctx", "head")
    return jax.shard_map(
        functools.partial(body, mesh.shape["ctx"], mesh.shape["head"]),
        mesh=mesh,
        in_specs=(both, both, both, P("head"), P("ctx"), P("head"), both),
        out_specs=(both,) * 4,
        check_vma=False,
    )
```

```python
import functools

import jax
import jax.numpy as jnp
from jax import lax
from jax.experimental import pallas as pl
from jax.experimental.pallas import tpu as pltpu
from jax.sharding import PartitionSpec as P

HEADS = 64
DH = 128
CHUNK = 128
AHEAD = 2
AHEAD_GRADS = 3
EPSILON = 1e-06
MESH = pl.DeviceIdType.MESH
F32 = jnp.float32
BF16 = jnp.bfloat16


def dot(a, b, da, db):
    return lax.dot_general(a, b, (((da,), (db,)), ((), ())), preferred_element_type=F32)


def kernel(
    shards, steps, peers, total,
    q_hbm, k_hbm, v_hbm, g_hbm, rate_hbm, starts_hbm, gain_hbm,
    n_out, gq_out, gk_out, gv_out,
    rate_ref, starts_ref, gain_ref,
    qs, ks, vs, gs, qw, att, ga, weights, gkp, gvp,
    joined, in_mask, out_mask, clear, d_state, full_state, d_grad,
    own, got, pre, flags_buf, kept_buf, sq_acc, cr_acc, inv_full, coef_full, x_buf,
    small_sem, in_sem, s_send, s_recv, f_send, f_recv, x_send, x_recv,
):
    heads, rows, _ = qs.shape
    chunks = rows // CHUNK
    ctx = lax.axis_index("ctx")
    me = lax.axis_index("head")

    def cols(h):
        return pl.ds(pl.multiple_of(h * DH, DH), DH)

    def load(i, h):
        hbm, buf = ((k_hbm, ks), (v_hbm, vs), (q_hbm, qs), (g_hbm, gs))[i]
        return pltpu.make_async_copy(hbm.at[:, cols(h)], buf.at[h], in_sem.at[i, h])

    def size_of(late, step):
        return 1 << (steps - 1 - step if late else step)

    def scan_copy(which, step, h, late):
        size = size_of(late, step)
        return pltpu.make_async_remote_copy(
            src_ref=own.at[which, step, h],
            dst_ref=got.at[which, step, h],
            send_sem=s_send.at[which, step, h],
            recv_sem=s_recv.at[which, step, h],
            device_id=(ctx + size - 2 * size * ((ctx // size) % 2), me),
            device_id_type=MESH,
        )

    def flag_copy(k):
        return pltpu.make_async_remote_copy(
            src_ref=flags_buf.at[ctx],
            dst_ref=flags_buf.at[ctx],
            send_sem=f_send.at[k],
            recv_sem=f_recv.at[k],
            device_id=((ctx + k) % shards, me),
            device_id_type=MESH,
        )

    def swap_copy(k):
        return pltpu.make_async_remote_copy(
            src_ref=x_buf.at[0],
            dst_ref=x_buf.at[k],
            send_sem=x_send.at[k],
            recv_sem=x_recv.at[k],
            device_id=(ctx, (me + k) % peers),
            device_id_type=MESH,
        )

    barrier = pltpu.get_barrier_semaphore()
    for k in range(1, shards):
        pl.semaphore_signal(
            barrier, inc=1, device_id=((ctx + k) % shards, me), device_id_type=MESH
        )

    def greet(k, c):
        pl.semaphore_signal(
            barrier, inc=1, device_id=(ctx, (me + k) % peers), device_id_type=MESH
        )
        return c

    lax.fori_loop(1, peers, greet, 0)

    small = [
        pltpu.make_async_copy(hbm, inside, small_sem.at[i])
        for i, (hbm, inside) in enumerate(
            ((starts_hbm, starts_ref), (rate_hbm, rate_ref), (gain_hbm, gain_ref))
        )
    ]
    for copy in small:
        copy.start()

    def start_loads(pair):
        def go(h, c):
            for i in pair:
                load(i, h).start()
            return c
        lax.fori_loop(0, heads, go, 0)

    start_loads((0, 1))
    start_loads((2, 3))
    small[0].wait()

    row_at = lax.broadcasted_iota(jnp.int32, (CHUNK, CHUNK), 0)
    col_at = lax.broadcasted_iota(jnp.int32, (CHUNK, CHUNK), 1)
    lower = row_at >= col_at
    ones_low = jnp.where(lower, 1.0, 0.0).astype(BF16)
    for c in range(chunks):
        flags = starts_ref[:, c * CHUNK:(c + 1) * CHUNK].astype(F32)
        wide = jnp.broadcast_to(flags, (DH, CHUNK)).astype(BF16)
        run_row = dot(wide, ones_low, 1, 1)[0:1, :]
        run_col = dot(ones_low, wide, 1, 1)
        count = jnp.sum(flags, axis=1, keepdims=True)
        both = jnp.concatenate([run_col] * (CHUNK // DH), axis=1)
        joined[c] = jnp.where(lower & (both == run_row), 1.0, 0.0)
        in_mask[c] = jnp.where(run_col == 0.0, 1.0, 0.0)
        out_mask[c] = jnp.where(run_col == count, 1.0, 0.0)
        clear[c] = jnp.broadcast_to(jnp.where(count == 0.0, 1.0, 0.0), (8, DH))
    whole = jnp.sum(starts_ref[...].astype(F32), axis=1, keepdims=True)
    flags_buf[ctx] = jnp.broadcast_to(jnp.where(whole == 0.0, 1.0, 0.0), (8, DH))

    place = lax.broadcasted_iota(jnp.int32, (CHUNK, DH), 0).astype(F32)
    gap = jnp.maximum(row_at - col_at, 0).astype(F32)

    def reach_in(rate):
        return jnp.exp(-rate * (place + 1.0))

    def reach_out(rate):
        return jnp.exp(-rate * (CHUNK - 1.0 - place))

    def carry(rate, c):
        return clear[c] * jnp.exp(jnp.full((8, DH), -rate * CHUNK, F32))

    def needs(which, late, step):
        at = shards - 1 - ctx if which else ctx
        size = size_of(late, step)
        upper = (at // size) % 2 == 1
        above = at // (2 * size)
        both = (above > 0) if late else (above < shards // (2 * size) - 1)
        return ~upper | both, upper | both

    def send_part(which, step, h, late):
        @pl.when(needs(which, late, step)[0])
        def _():
            scan_copy(which, step, h, late).start()

    table = {}

    def factor(which, first, last, use, other):
        kept = jnp.ones((8, DH), F32)
        for i in range(shards):
            flag = flags_buf[shards - 1 - i if which else i]
            kept = kept * jnp.where((i >= first) & (i < last), flag, 1.0)
        slot = sum(len(entry) for entry in table.values())
        kept_buf[slot] = jnp.where(use, kept, other)
        return slot, jnp.where(use, jnp.maximum(last - first, 0) * rows, 0).astype(F32)

    def make_table():
        for which in range(2):
            at = shards - 1 - ctx if which else ctx
            for late in (False, True):
                for step in range(steps):
                    size = size_of(late, step)
                    start = at - at % (2 * size)
                    middle, end, upper = start + size, start + 2 * size, at >= start + size
                    key = (which, late, step)
                    table[key] = []
                    if not late:
                        entries = [(middle, at, upper, 0.0), (middle, end, ~upper, 1.0), (middle, end, upper, 1.0)]
                    else:
                        size = size_of(late, min(step + 1, steps - 1))
                        begin = at - at % (2 * size)
                        half = begin + size
                        lower = at < half
                        first = (at - middle + start + 1, middle, upper, 0.0) if step == 0 else (start, middle, upper, 1.0)
                        entries = [first, (begin, half, lower, 1.0), (at + 1, half, lower, 0.0)]
                    for entry in entries[:1] if step == steps - 1 else entries:
                        table[key] = table[key] + [factor(which, *entry)]

    def put(which, h, late, state):
        own[which, 0, h] = state
        send_part(which, 0, h, late)

    def await_part(which, step, h, late):
        @pl.when(needs(which, late, step)[1])
        def _():
            scan_copy(which, step, h, late).wait_recv()

    def take(which, step, h, late, rate):
        needed = needs(which, late, step)[1]
        factors = [
            (kept_buf[slot] * jnp.exp(jnp.full((8, DH), -rate * length, F32)))[0:1, :]
            for slot, length in table[which, late, step]
        ]
        came = jnp.where(needed, got[which, step, h], 0.0)
        if not late:
            state = factors[0] * came
            if step > 0:
                state = state + pre[h]
        else:
            state = factors[0] * (came if step == 0 else pre[h])
            if step > 0:
                state = state + came
        if step == steps - 1:
            return state
        pre[h] = state
        own[which, step + 1, h] = (
            factors[1] * state + factors[2] * own[which, 0, h]
            if late
            else factors[1] * own[which, step, h] + factors[2] * came
        )
        send_part(which, step + 1, h, late)
        return None

    def take_pair(which, j):
        for step in range(steps - 1):
            for late in (False, True):
                await_part(which, step, 2 * j + int(late), late)
            for late in (False, True):
                h = 2 * j + int(late)
                take(which, step, h, late, rate_ref[h])

    def finish_pairs(which, work):
        def go(j, carried):
            for late in (False, True):
                await_part(which, steps - 1, 2 * j + int(late), late)
            for late in (False, True):
                work(2 * j + int(late), late)
            return carried
        lax.fori_loop(0, heads // 2, go, 0)

    def pairs(work):
        def go(j, carried):
            for late in (False, True):
                work(2 * j + int(late), late)
            return carried
        lax.fori_loop(0, heads // 2, go, 0)

    def part(c):
        return slice(c * CHUNK, (c + 1) * CHUNK)

    small[1].wait()
    small[2].wait()
    pl.semaphore_wait(barrier, shards + peers - 2)
    for k in range(1, shards):
        flag_copy(k).start()

    def make_states(h, late):
        load(0, h).wait()
        load(1, h).wait()
        rate = rate_ref[h]
        out = reach_out(rate)
        state = jnp.zeros((DH, DH), F32)
        for c in range(chunks):
            weighted = (ks[h, part(c), :].astype(F32) * (out * out_mask[c])).astype(BF16)
            add = dot(weighted, vs[h, part(c), :], 0, 0)
            d_state[h, c] = add
            keep = carry(rate, c)
            state = keep[0:1, :] * state + add
        put(0, h, late, state)

    pairs(make_states)
    sq_acc[...] = jnp.zeros_like(sq_acc)
    cr_acc[...] = jnp.zeros_like(cr_acc)
    for k in range(1, shards):
        flag_copy(k).wait_recv()
    make_table()

    def attend(h):
        load(2, h).wait()
        load(3, h).wait()
        decay = jnp.exp(-rate_ref[h] * gap)
        reach = reach_in(rate_ref[h])
        def raw(c):
            return dot(qs[h, part(c), :], ks[h, part(c), :], 1, 1)

        ready = [raw(c) for c in range(min(AHEAD, chunks))]
        for c in range(chunks):
            scores = ready.pop(0)
            if c + AHEAD < chunks:
                ready.append(raw(c + AHEAD))
            w = (scores * (decay * joined[c])).astype(BF16)
            weights[h, c] = jnp.transpose(w)
            att[h, part(c), :] = dot(w, vs[h, part(c), :], 1, 0)
            qw[h, part(c), :] = (qs[h, part(c), :].astype(F32) * (reach * in_mask[c])).astype(BF16)

    def attend_pair(j, carried):
        attend(2 * j)
        attend(2 * j + 1)
        take_pair(0, j)
        return carried

    lax.fori_loop(0, heads // 2, attend_pair, 0)

    def finish_attend(h, late):
        rate = rate_ref[h]
        state = take(0, steps - 1, h, late, rate)
        reach = reach_in(rate)
        gain = gain_ref[pl.ds(h, 1), :]
        for c in range(chunks):
            small = state.astype(BF16)
            full_state[h, c] = small
            a = att[h, part(c), :] + (reach * in_mask[c]) * dot(qs[h, part(c), :], small, 1, 0)
            att[h, part(c), :] = a
            sq_acc[part(c), :] += a * a
            cr_acc[part(c), :] += gs[h, part(c), :].astype(F32) * gain * a
            if c < chunks - 1:
                state = carry(rate, c)[0:1, :] * state + d_state[h, c]

    finish_pairs(0, finish_attend)

    x_buf[0, 0:1, :] = jnp.sum(jnp.transpose(sq_acc[...]), axis=0, keepdims=True)
    x_buf[0, 1:2, :] = jnp.sum(jnp.transpose(cr_acc[...]), axis=0, keepdims=True)

    def send(k, c):
        swap_copy(k).start()
        return c

    lax.fori_loop(1, peers, send, 0)

    def receive(k, c):
        swap_copy(k).wait_recv()
        return c + x_buf[k]

    sums = lax.fori_loop(1, peers, receive, x_buf[0])
    inverse = 1.0 / jnp.sqrt(sums[0:1, :] / total + EPSILON)
    coef = inverse * inverse * inverse * (sums[1:2, :] / total)
    inv_full[...] = jnp.transpose(jnp.broadcast_to(inverse, (DH, rows)))
    coef_full[...] = jnp.transpose(jnp.broadcast_to(coef, (DH, rows)))

    def make_grads(h, late):
        rate = rate_ref[h]
        gain = gain_ref[pl.ds(h, 1), :]
        state = jnp.zeros((DH, DH), F32)
        for c in reversed(range(chunks)):
            a, inv = att[h, part(c), :], inv_full[part(c), :]
            gained = gs[h, part(c), :].astype(F32) * gain
            grad = (inv * gained - a * coef_full[part(c), :]).astype(BF16)
            ga[h, part(c), :] = grad
            add = dot(qw[h, part(c), :], grad, 0, 0)
            d_grad[h, c] = add
            keep = carry(rate, c)
            state = keep[0:1, :] * state + add
        put(1, h, late, state)

    pairs(make_grads)

    def inner_grads(h):
        rate = rate_ref[h]
        decay = jnp.exp(-rate * gap)
        reach = reach_in(rate)
        gain = gain_ref[pl.ds(h, 1), :]
        def raw(c):
            grad = ga[h, part(c), :]
            return dot(grad, vs[h, part(c), :], 1, 1), dot(grad, full_state[h, c], 1, 1)

        ready = [raw(c) for c in range(min(AHEAD_GRADS, chunks))]
        for c in range(chunks):
            wide, far = ready.pop(0)
            if c + AHEAD_GRADS < chunks:
                ready.append(raw(c + AHEAD_GRADS))
            n_out[part(c), cols(h)] = (att[h, part(c), :] * inv_full[part(c), :] * gain).astype(BF16)
            gvp[h, part(c), :] = dot(weights[h, c], ga[h, part(c), :], 1, 0)
            d = (wide * (decay * joined[c])).astype(BF16)
            gq = dot(d, ks[h, part(c), :], 1, 0) + (reach * in_mask[c]) * far
            gq_out[part(c), cols(h)] = gq.astype(BF16)
            gkp[h, part(c), :] = dot(d, qs[h, part(c), :], 0, 0)

    def inner_pair(j, carried):
        take_pair(1, j)
        inner_grads(2 * j)
        inner_grads(2 * j + 1)
        return carried

    lax.fori_loop(0, heads // 2, inner_pair, 0)

    def finish_grads(h, late):
        rate = rate_ref[h]
        state = take(1, steps - 1, h, late, rate)
        out = reach_out(rate)
        for c in reversed(range(chunks)):
            small = state.astype(BF16)
            reach = out * out_mask[c]
            gk = gkp[h, part(c), :] + reach * dot(vs[h, part(c), :], small, 1, 1)
            gv = gvp[h, part(c), :] + reach * dot(ks[h, part(c), :], small, 1, 0)
            gk_out[part(c), cols(h)] = gk.astype(BF16)
            gv_out[part(c), cols(h)] = gv.astype(BF16)
            if c > 0:
                state = carry(rate, c)[0:1, :] * state + d_grad[h, c]

    finish_pairs(1, finish_grads)

    def drain(h, late):
        for which in range(2):
            for step in range(steps):
                @pl.when(needs(which, late, step)[0])
                def _():
                    scan_copy(which, step, h, late).wait_send()

    pairs(drain)
    for k in range(1, shards):
        flag_copy(k).wait_send()

    def drain_swaps(k, c):
        swap_copy(k).wait_send()
        return c

    lax.fori_loop(1, peers, drain_swaps, 0)


def write_out(*refs):
    sems = refs[8]
    copies = [pltpu.make_async_copy(refs[i], refs[i + 4], sems.at[i]) for i in range(4)]
    for copy in copies:
        copy.start()
    for copy in copies:
        copy.wait()


def body(shards, peers, query_rows, key_rows, value_rows, decay_rate, starts, norm_gain, grad_out):
    rows, features = query_rows.shape
    heads = features // DH
    chunks = rows // CHUNK
    steps = (shards - 1).bit_length()
    big = jax.ShapeDtypeStruct((rows, features), BF16)
    whole = pl.BlockSpec(memory_space=pltpu.HBM)
    inside = pl.BlockSpec(memory_space=pltpu.VMEM)

    def head_rows(dtype):
        return pltpu.VMEM((heads, rows, DH), dtype)

    dma = pltpu.SemaphoreType.DMA
    kept = pl.pallas_call(
        functools.partial(kernel, shards, steps, peers, HEADS * DH),
        out_shape=(pltpu.VMEM((rows, features), BF16),) * 4,
        in_specs=[whole] * 7,
        out_specs=(inside,) * 4,
        scratch_shapes=[
            pltpu.SMEM((heads,), F32),
            pltpu.VMEM((1, rows), jnp.int32),
            pltpu.VMEM((heads, DH), F32),
        ]
        + [head_rows(BF16)] * 5
        + [head_rows(F32), head_rows(BF16), pltpu.VMEM((heads, chunks, CHUNK, CHUNK), BF16)]
        + [head_rows(F32)] * 2
        + [
            pltpu.VMEM((chunks, CHUNK, CHUNK), F32),
            pltpu.VMEM((chunks, CHUNK, DH), F32),
            pltpu.VMEM((chunks, CHUNK, DH), F32),
            pltpu.VMEM((chunks, 8, DH), F32),
            pltpu.VMEM((heads, chunks, DH, DH), F32),
            pltpu.VMEM((heads, chunks, DH, DH), BF16),
            pltpu.VMEM((heads, chunks, DH, DH), F32),
            pltpu.VMEM((2, steps, heads, DH, DH), F32),
            pltpu.VMEM((2, steps, heads, DH, DH), F32),
            pltpu.VMEM((heads, DH, DH), F32),
            pltpu.VMEM((shards, 8, DH), F32),
            pltpu.VMEM((12 * steps, 8, DH), F32),
            pltpu.VMEM((rows, DH), F32),
            pltpu.VMEM((rows, DH), F32),
            pltpu.VMEM((rows, DH), F32),
            pltpu.VMEM((rows, DH), F32),
            pltpu.VMEM((peers, 2, rows), F32),
            dma((3,)),
            dma((4, heads)),
            dma((2, steps, heads)),
            dma((2, steps, heads)),
            dma((shards,)),
            dma((shards,)),
            dma((peers,)),
            dma((peers,)),
        ],
        compiler_params=pltpu.CompilerParams(
            collective_id=0, has_side_effects=True, vmem_limit_bytes=55 * 1024 * 1024
        ),
    )(
        query_rows, key_rows, value_rows, grad_out, decay_rate,
        starts.reshape(1, rows), norm_gain.reshape(heads, DH),
    )
    return pl.pallas_call(
        write_out,
        out_shape=(big,) * 4,
        in_specs=[pl.BlockSpec(memory_space=pl.ANY)] * 4,
        out_specs=(whole,) * 4,
        scratch_shapes=[dma((4,))],
        compiler_params=pltpu.CompilerParams(vmem_limit_bytes=1024 * 1024),
    )(*kept)


def solution(mesh):
    both = P("ctx", "head")
    return jax.shard_map(
        functools.partial(body, mesh.shape["ctx"], mesh.shape["head"]),
        mesh=mesh,
        in_specs=(both, both, both, P("head"), P("ctx"), P("head"), both),
        out_specs=(both,) * 4,
        check_vma=False,
    )
```

```python
import functools

import jax
import jax.numpy as jnp
from jax import lax
from jax.experimental import pallas as pl
from jax.experimental.pallas import tpu as pltpu
from jax.sharding import PartitionSpec as P

HEADS = 64
DH = 128
CHUNK = 128
AHEAD = 2
AHEAD_GRADS = 3
EPSILON = 1e-06
MESH = pl.DeviceIdType.MESH
F32 = jnp.float32
BF16 = jnp.bfloat16


def dot(a, b, da, db):
    return lax.dot_general(a, b, (((da,), (db,)), ((), ())), preferred_element_type=F32)


def kernel(
    shards, steps, peers, total,
    q_hbm, k_hbm, v_hbm, g_hbm, rate_hbm, starts_hbm, gain_hbm,
    n_out, gq_out, gkp, gvp, ks, vs, d_grad, last, out_mask, clear, rate_rows,
    rate_ref, starts_ref, gain_ref,
    qs, gs, qw, att, ga, weights,
    joined, in_mask, d_state, full_state,
    own, got, pre, flags_buf, kept_buf, sq_acc, cr_acc, inv_full, coef_full, x_buf,
    small_sem, in_sem, s_send, s_recv, f_send, f_recv, x_send, x_recv,
):
    heads, rows, _ = qs.shape
    chunks = rows // CHUNK
    ctx = lax.axis_index("ctx")
    me = lax.axis_index("head")

    def cols(h):
        return pl.ds(pl.multiple_of(h * DH, DH), DH)

    def load(i, h):
        hbm, buf = ((k_hbm, ks), (v_hbm, vs), (q_hbm, qs), (g_hbm, gs))[i]
        return pltpu.make_async_copy(hbm.at[:, cols(h)], buf.at[h], in_sem.at[i, h])

    def size_of(late, step):
        return 1 << (steps - 1 - step if late else step)

    def scan_copy(which, step, h, late):
        size = size_of(late, step)
        return pltpu.make_async_remote_copy(
            src_ref=own.at[which, step, h],
            dst_ref=got.at[which, step, h],
            send_sem=s_send.at[which, step, h],
            recv_sem=s_recv.at[which, step, h],
            device_id=(ctx + size - 2 * size * ((ctx // size) % 2), me),
            device_id_type=MESH,
        )

    def flag_copy(k):
        return pltpu.make_async_remote_copy(
            src_ref=flags_buf.at[ctx],
            dst_ref=flags_buf.at[ctx],
            send_sem=f_send.at[k],
            recv_sem=f_recv.at[k],
            device_id=((ctx + k) % shards, me),
            device_id_type=MESH,
        )

    def across(k):
        other = me
        for bit in range(peers.bit_length()):
            size = 1 << bit
            if k & size:
                other = other + size - 2 * size * ((me // size) % 2)
        return other

    def swap_copy(k):
        return pltpu.make_async_remote_copy(
            src_ref=x_buf.at[0],
            dst_ref=x_buf.at[k],
            send_sem=x_send.at[k],
            recv_sem=x_recv.at[k],
            device_id=(ctx, across(k)),
            device_id_type=MESH,
        )

    barrier = pltpu.get_barrier_semaphore()
    for k in range(1, shards):
        pl.semaphore_signal(
            barrier, inc=1, device_id=((ctx + k) % shards, me), device_id_type=MESH
        )

    def greet(k, c):
        pl.semaphore_signal(
            barrier, inc=1, device_id=(ctx, (me + k) % peers), device_id_type=MESH
        )
        return c

    lax.fori_loop(1, peers, greet, 0)

    small = [
        pltpu.make_async_copy(hbm, inside, small_sem.at[i])
        for i, (hbm, inside) in enumerate(
            ((starts_hbm, starts_ref), (rate_hbm, rate_ref), (gain_hbm, gain_ref))
        )
    ]
    for copy in small:
        copy.start()

    def start_loads(pair):
        def go(h, c):
            for i in pair:
                load(i, h).start()
            return c
        lax.fori_loop(0, heads, go, 0)

    start_loads((0, 1))
    start_loads((2, 3))
    small[0].wait()

    row_at = lax.broadcasted_iota(jnp.int32, (CHUNK, CHUNK), 0)
    col_at = lax.broadcasted_iota(jnp.int32, (CHUNK, CHUNK), 1)
    lower = row_at >= col_at
    ones_low = jnp.where(lower, 1.0, 0.0).astype(BF16)
    for c in range(chunks):
        flags = starts_ref[:, c * CHUNK:(c + 1) * CHUNK].astype(F32)
        wide = jnp.broadcast_to(flags, (DH, CHUNK)).astype(BF16)
        run_row = dot(wide, ones_low, 1, 1)[0:1, :]
        run_col = dot(ones_low, wide, 1, 1)
        count = jnp.sum(flags, axis=1, keepdims=True)
        both = jnp.concatenate([run_col] * (CHUNK // DH), axis=1)
        joined[c] = jnp.where(lower & (both == run_row), 1.0, 0.0)
        in_mask[c] = jnp.where(run_col == 0.0, 1.0, 0.0)
        out_mask[c] = jnp.where(run_col == count, 1.0, 0.0)
        clear[c] = jnp.broadcast_to(jnp.where(count == 0.0, 1.0, 0.0), (8, DH))
    whole = jnp.sum(starts_ref[...].astype(F32), axis=1, keepdims=True)
    flags_buf[ctx] = jnp.broadcast_to(jnp.where(whole == 0.0, 1.0, 0.0), (8, DH))

    place = lax.broadcasted_iota(jnp.int32, (CHUNK, DH), 0).astype(F32)
    gap = jnp.maximum(row_at - col_at, 0).astype(F32)

    def reach_in(rate):
        return jnp.exp(-rate * (place + 1.0))

    def reach_out(rate):
        return jnp.exp(-rate * (CHUNK - 1.0 - place))

    def carry(rate, c):
        return clear[c] * jnp.exp(jnp.full((8, DH), -rate * CHUNK, F32))

    def spread(h, c):
        rate_rows[h] = jnp.full((8, DH), rate_ref[h], F32)
        return c

    def needs(which, late, step):
        at = shards - 1 - ctx if which else ctx
        size = size_of(late, step)
        upper = (at // size) % 2 == 1
        above = at // (2 * size)
        both = (above > 0) if late else (above < shards // (2 * size) - 1)
        return ~upper | both, upper | both

    def send_part(which, step, h, late):
        @pl.when(needs(which, late, step)[0])
        def _():
            scan_copy(which, step, h, late).start()

    table = {}

    def factor(which, first, last, use, other):
        kept = jnp.ones((8, DH), F32)
        for i in range(shards):
            flag = flags_buf[shards - 1 - i if which else i]
            kept = kept * jnp.where((i >= first) & (i < last), flag, 1.0)
        slot = sum(len(entry) for entry in table.values())
        kept_buf[slot] = jnp.where(use, kept, other)
        return slot, jnp.where(use, jnp.maximum(last - first, 0) * rows, 0).astype(F32)

    def make_table():
        for which in range(2):
            at = shards - 1 - ctx if which else ctx
            for late in (False, True):
                for step in range(steps):
                    size = size_of(late, step)
                    start = at - at % (2 * size)
                    middle, end, upper = start + size, start + 2 * size, at >= start + size
                    key = (which, late, step)
                    table[key] = []
                    if not late:
                        entries = [(middle, at, upper, 0.0), (middle, end, ~upper, 1.0), (middle, end, upper, 1.0)]
                    else:
                        size = size_of(late, min(step + 1, steps - 1))
                        begin = at - at % (2 * size)
                        half = begin + size
                        lower = at < half
                        first = (at - middle + start + 1, middle, upper, 0.0) if step == 0 else (start, middle, upper, 1.0)
                        entries = [first, (begin, half, lower, 1.0), (at + 1, half, lower, 0.0)]
                    for entry in entries[:1] if step == steps - 1 else entries:
                        table[key] = table[key] + [factor(which, *entry)]

    def put(which, h, late, state):
        own[which, 0, h] = state
        send_part(which, 0, h, late)

    def await_part(which, step, h, late):
        @pl.when(needs(which, late, step)[1])
        def _():
            scan_copy(which, step, h, late).wait_recv()

    def take(which, step, h, late, rate):
        needed = needs(which, late, step)[1]
        factors = [
            (kept_buf[slot] * jnp.exp(jnp.full((8, DH), -rate * length, F32)))[0:1, :]
            for slot, length in table[which, late, step]
        ]
        came = jnp.where(needed, got[which, step, h], 0.0)
        if not late:
            state = factors[0] * came
            if step > 0:
                state = state + pre[h]
        else:
            state = factors[0] * (came if step == 0 else pre[h])
            if step > 0:
                state = state + came
        if step == steps - 1:
            return state
        pre[h] = state
        own[which, step + 1, h] = (
            factors[1] * state + factors[2] * own[which, 0, h]
            if late
            else factors[1] * own[which, step, h] + factors[2] * came
        )
        send_part(which, step + 1, h, late)
        return None

    def take_pair(which, j):
        for step in range(steps - 1):
            for late in (False, True):
                await_part(which, step, 2 * j + int(late), late)
            for late in (False, True):
                h = 2 * j + int(late)
                take(which, step, h, late, rate_ref[h])

    def finish_pairs(which, work):
        def go(j, carried):
            for late in (False, True):
                await_part(which, steps - 1, 2 * j + int(late), late)
            for late in (False, True):
                work(2 * j + int(late), late)
            return carried
        lax.fori_loop(0, heads // 2, go, 0)

    def pairs(work):
        def go(j, carried):
            for late in (False, True):
                work(2 * j + int(late), late)
            return carried
        lax.fori_loop(0, heads // 2, go, 0)

    def part(c):
        return slice(c * CHUNK, (c + 1) * CHUNK)

    small[1].wait()
    small[2].wait()
    lax.fori_loop(0, heads, spread, 0)
    pl.semaphore_wait(barrier, shards + peers - 2)
    for k in range(1, shards):
        flag_copy(k).start()

    def make_states(h, late):
        load(0, h).wait()
        load(1, h).wait()
        rate = rate_ref[h]
        out = reach_out(rate)
        state = jnp.zeros((DH, DH), F32)
        for c in range(chunks):
            weighted = (ks[h, part(c), :].astype(F32) * (out * out_mask[c])).astype(BF16)
            add = dot(weighted, vs[h, part(c), :], 0, 0)
            d_state[h, c] = add
            keep = carry(rate, c)
            state = keep[0:1, :] * state + add
        put(0, h, late, state)

    pairs(make_states)
    sq_acc[...] = jnp.zeros_like(sq_acc)
    cr_acc[...] = jnp.zeros_like(cr_acc)
    for k in range(1, shards):
        flag_copy(k).wait_recv()
    make_table()

    def attend(h):
        load(2, h).wait()
        load(3, h).wait()
        decay = jnp.exp(-rate_ref[h] * gap)
        reach = reach_in(rate_ref[h])
        def raw(c):
            return dot(qs[h, part(c), :], ks[h, part(c), :], 1, 1)

        ready = [raw(c) for c in range(min(AHEAD, chunks))]
        for c in range(chunks):
            scores = ready.pop(0)
            if c + AHEAD < chunks:
                ready.append(raw(c + AHEAD))
            w = (scores * (decay * joined[c])).astype(BF16)
            weights[h, c] = jnp.transpose(w)
            att[h, part(c), :] = dot(w, vs[h, part(c), :], 1, 0)
            qw[h, part(c), :] = (qs[h, part(c), :].astype(F32) * (reach * in_mask[c])).astype(BF16)

    def attend_pair(j, carried):
        attend(2 * j)
        attend(2 * j + 1)
        take_pair(0, j)
        return carried

    lax.fori_loop(0, heads // 2, attend_pair, 0)

    def finish_attend(h, late):
        rate = rate_ref[h]
        state = take(0, steps - 1, h, late, rate)
        reach = reach_in(rate)
        gain = gain_ref[pl.ds(h, 1), :]
        for c in range(chunks):
            small = state.astype(BF16)
            full_state[h, c] = small
            a = att[h, part(c), :] + (reach * in_mask[c]) * dot(qs[h, part(c), :], small, 1, 0)
            att[h, part(c), :] = a
            sq_acc[part(c), :] += a * a
            cr_acc[part(c), :] += gs[h, part(c), :].astype(F32) * gain * a
            if c < chunks - 1:
                state = carry(rate, c)[0:1, :] * state + d_state[h, c]

    finish_pairs(0, finish_attend)

    x_buf[0, 0:1, :] = jnp.sum(jnp.transpose(sq_acc[...]), axis=0, keepdims=True)
    x_buf[0, 1:2, :] = jnp.sum(jnp.transpose(cr_acc[...]), axis=0, keepdims=True)

    for k in reversed(range(1, peers)):
        swap_copy(k).start()
    sums = x_buf[0]
    for k in range(1, peers):
        swap_copy(k).wait_recv()
        sums = sums + x_buf[k]
    inverse = 1.0 / jnp.sqrt(sums[0:1, :] / total + EPSILON)
    coef = inverse * inverse * inverse * (sums[1:2, :] / total)
    inv_full[...] = jnp.transpose(jnp.broadcast_to(inverse, (DH, rows)))
    coef_full[...] = jnp.transpose(jnp.broadcast_to(coef, (DH, rows)))

    def make_grads(h, late):
        rate = rate_ref[h]
        gain = gain_ref[pl.ds(h, 1), :]
        state = jnp.zeros((DH, DH), F32)
        for c in reversed(range(chunks)):
            a, inv = att[h, part(c), :], inv_full[part(c), :]
            gained = gs[h, part(c), :].astype(F32) * gain
            grad = (inv * gained - a * coef_full[part(c), :]).astype(BF16)
            ga[h, part(c), :] = grad
            add = dot(qw[h, part(c), :], grad, 0, 0)
            d_grad[h, c] = add
            keep = carry(rate, c)
            state = keep[0:1, :] * state + add
        put(1, h, late, state)

    pairs(make_grads)

    def inner_grads(h):
        rate = rate_ref[h]
        decay = jnp.exp(-rate * gap)
        reach = reach_in(rate)
        gain = gain_ref[pl.ds(h, 1), :]
        def raw(c):
            grad = ga[h, part(c), :]
            return dot(grad, vs[h, part(c), :], 1, 1), dot(grad, full_state[h, c], 1, 1)

        ready = [raw(c) for c in range(min(AHEAD_GRADS, chunks))]
        for c in range(chunks):
            wide, far = ready.pop(0)
            if c + AHEAD_GRADS < chunks:
                ready.append(raw(c + AHEAD_GRADS))
            n_out[part(c), cols(h)] = (att[h, part(c), :] * inv_full[part(c), :] * gain).astype(BF16)
            gvp[h, part(c), :] = dot(weights[h, c], ga[h, part(c), :], 1, 0)
            d = (wide * (decay * joined[c])).astype(BF16)
            gq = dot(d, ks[h, part(c), :], 1, 0) + (reach * in_mask[c]) * far
            gq_out[part(c), cols(h)] = gq.astype(BF16)
            gkp[h, part(c), :] = dot(d, qs[h, part(c), :], 0, 0)

    def inner_pair(j, carried):
        take_pair(1, j)
        inner_grads(2 * j)
        inner_grads(2 * j + 1)
        return carried

    lax.fori_loop(0, heads // 2, inner_pair, 0)

    def keep_last(h, late):
        last[h] = take(1, steps - 1, h, late, rate_ref[h])

    finish_pairs(1, keep_last)

    def drain(h, late):
        for which in range(2):
            for step in range(steps):
                @pl.when(needs(which, late, step)[0])
                def _():
                    scan_copy(which, step, h, late).wait_send()

    pairs(drain)
    for k in range(1, shards):
        flag_copy(k).wait_send()

    for k in range(1, peers):
        swap_copy(k).wait_send()


def write_out(
    n_in, gq_in, gkp, gvp, ks, vs, d_grad, last, out_mask, clear, rate_rows,
    n_out, gq_out, gk_out, gv_out, gk, gv, sems, pair_sems,
):
    heads, rows, _ = ks.shape
    copies = [
        pltpu.make_async_copy(n_in, n_out, sems.at[0]),
        pltpu.make_async_copy(gq_in, gq_out, sems.at[1]),
    ]
    for copy in copies:
        copy.start()
    place = lax.broadcasted_iota(jnp.int32, (CHUNK, DH), 0).astype(F32)

    def pair_copies(j):
        width = gk.shape[1] // (heads // 2)
        cols = pl.ds(pl.multiple_of(j * width, width), width)
        return [
            pltpu.make_async_copy(gk.at[:, cols], gk_out.at[:, cols], pair_sems.at[0, j]),
            pltpu.make_async_copy(gv.at[:, cols], gv_out.at[:, cols], pair_sems.at[1, j]),
        ]

    def finish(h):
        cols = pl.ds(pl.multiple_of(h * DH, DH), DH)
        rate = rate_rows[h]
        out = jnp.exp(-rate[0:1, :] * (CHUNK - 1.0 - place))
        fade = jnp.exp(-rate * CHUNK)
        state = last[h]
        for c in reversed(range(rows // CHUNK)):
            part = slice(c * CHUNK, (c + 1) * CHUNK)
            small = state.astype(BF16)
            reach = out * out_mask[c]
            gk[part, cols] = (gkp[h, part, :] + reach * dot(vs[h, part, :], small, 1, 1)).astype(BF16)
            gv[part, cols] = (gvp[h, part, :] + reach * dot(ks[h, part, :], small, 1, 0)).astype(BF16)
            if c > 0:
                state = (clear[c] * fade)[0:1, :] * state + d_grad[h, c]

    def go(j, carried):
        finish(2 * j)
        finish(2 * j + 1)
        for copy in pair_copies(j):
            copy.start()
        return carried

    lax.fori_loop(0, heads // 2, go, 0)

    def drain(j, carried):
        for copy in pair_copies(j):
            copy.wait()
        return carried

    lax.fori_loop(0, heads // 2, drain, 0)
    for copy in copies:
        copy.wait()


def body(shards, peers, query_rows, key_rows, value_rows, decay_rate, starts, norm_gain, grad_out):
    rows, features = query_rows.shape
    heads = features // DH
    chunks = rows // CHUNK
    steps = (shards - 1).bit_length()
    big = jax.ShapeDtypeStruct((rows, features), BF16)
    whole = pl.BlockSpec(memory_space=pltpu.HBM)
    inside = pl.BlockSpec(memory_space=pltpu.VMEM)

    def head_rows(dtype):
        return pltpu.VMEM((heads, rows, DH), dtype)

    dma = pltpu.SemaphoreType.DMA
    handed = (
        (pltpu.VMEM((rows, features), BF16),) * 2
        + (head_rows(F32),) * 2
        + (head_rows(BF16),) * 2
        + (
            pltpu.VMEM((heads, chunks, DH, DH), F32),
            pltpu.VMEM((heads, DH, DH), F32),
            pltpu.VMEM((chunks, CHUNK, DH), F32),
            pltpu.VMEM((chunks, 8, DH), F32),
            pltpu.VMEM((heads, 8, DH), F32),
        )
    )
    kept = pl.pallas_call(
        functools.partial(kernel, shards, steps, peers, HEADS * DH),
        out_shape=handed,
        in_specs=[whole] * 7,
        out_specs=(inside,) * len(handed),
        scratch_shapes=[
            pltpu.SMEM((heads,), F32),
            pltpu.VMEM((1, rows), jnp.int32),
            pltpu.VMEM((heads, DH), F32),
        ]
        + [head_rows(BF16)] * 3
        + [head_rows(F32), head_rows(BF16), pltpu.VMEM((heads, chunks, CHUNK, CHUNK), BF16)]
        + [
            pltpu.VMEM((chunks, CHUNK, CHUNK), F32),
            pltpu.VMEM((chunks, CHUNK, DH), F32),
            pltpu.VMEM((heads, chunks, DH, DH), F32),
            pltpu.VMEM((heads, chunks, DH, DH), BF16),
            pltpu.VMEM((2, steps, heads, DH, DH), F32),
            pltpu.VMEM((2, steps, heads, DH, DH), F32),
            pltpu.VMEM((heads, DH, DH), F32),
            pltpu.VMEM((shards, 8, DH), F32),
            pltpu.VMEM((12 * steps, 8, DH), F32),
            pltpu.VMEM((rows, DH), F32),
            pltpu.VMEM((rows, DH), F32),
            pltpu.VMEM((rows, DH), F32),
            pltpu.VMEM((rows, DH), F32),
            pltpu.VMEM((peers, 2, rows), F32),
            dma((3,)),
            dma((4, heads)),
            dma((2, steps, heads)),
            dma((2, steps, heads)),
            dma((shards,)),
            dma((shards,)),
            dma((peers,)),
            dma((peers,)),
        ],
        compiler_params=pltpu.CompilerParams(
            collective_id=0, has_side_effects=True, vmem_limit_bytes=34 * 1024 * 1024
        ),
    )(
        query_rows, key_rows, value_rows, grad_out, decay_rate,
        starts.reshape(1, rows), norm_gain.reshape(heads, DH),
    )
    return pl.pallas_call(
        write_out,
        out_shape=(big,) * 4,
        in_specs=[inside] * len(handed),
        out_specs=(whole,) * 4,
        scratch_shapes=[
            pltpu.VMEM((rows, features), BF16),
            pltpu.VMEM((rows, features), BF16),
            dma((2,)),
            dma((2, heads // 2)),
        ],
        compiler_params=pltpu.CompilerParams(vmem_limit_bytes=6 * 1024 * 1024),
    )(*kept)


def solution(mesh):
    both = P("ctx", "head")
    return jax.shard_map(
        functools.partial(body, mesh.shape["ctx"], mesh.shape["head"]),
        mesh=mesh,
        in_specs=(both, both, both, P("head"), P("ctx"), P("head"), both),
        out_specs=(both,) * 4,
        check_vma=False,
    )
```

```python
import functools

import jax
import jax.numpy as jnp
from jax import lax
from jax.experimental import pallas as pl
from jax.experimental.pallas import tpu as pltpu
from jax.sharding import PartitionSpec as P

HEADS = 64
DH = 128
CHUNK = 128
AHEAD = 2
AHEAD_GRADS = 3
EPSILON = 1e-06
MESH = pl.DeviceIdType.MESH
F32 = jnp.float32
BF16 = jnp.bfloat16


def dot(a, b, da, db):
    return lax.dot_general(a, b, (((da,), (db,)), ((), ())), preferred_element_type=F32)


def kernel(
    shards, steps, peers, total,
    q_hbm, k_hbm, v_hbm, g_hbm, rate_hbm, starts_hbm, gain_hbm,
    n_out, gq_out, gkp, gvp, ks, vs, d_grad, last, out_mask, clear, rate_rows,
    rate_ref, starts_ref, gain_ref,
    qs, gs, qw, att, ga, weights,
    joined, in_mask, d_state, full_state,
    own, got, pre, flags_buf, kept_buf, sq_acc, cr_acc, inv_full, coef_full, x_buf,
    small_sem, in_sem, s_send, s_recv, f_send, f_recv, x_send, x_recv,
):
    heads, rows, _ = qs.shape
    chunks = rows // CHUNK
    ctx = lax.axis_index("ctx")
    me = lax.axis_index("head")

    def cols(h):
        return pl.ds(pl.multiple_of(h * DH, DH), DH)

    def load(i, h):
        hbm, buf = ((k_hbm, ks), (v_hbm, vs), (q_hbm, qs), (g_hbm, gs))[i]
        return pltpu.make_async_copy(hbm.at[:, cols(h)], buf.at[h], in_sem.at[i, h])

    def size_of(late, step):
        return 1 << (steps - 1 - step if late else step)

    def scan_copy(which, step, h, late):
        size = size_of(late, step)
        return pltpu.make_async_remote_copy(
            src_ref=own.at[which, step, h],
            dst_ref=got.at[which, step, h],
            send_sem=s_send.at[which, step, h],
            recv_sem=s_recv.at[which, step, h],
            device_id=(ctx + size - 2 * size * ((ctx // size) % 2), me),
            device_id_type=MESH,
        )

    def flag_copy(k):
        return pltpu.make_async_remote_copy(
            src_ref=flags_buf.at[ctx],
            dst_ref=flags_buf.at[ctx],
            send_sem=f_send.at[k],
            recv_sem=f_recv.at[k],
            device_id=((ctx + k) % shards, me),
            device_id_type=MESH,
        )

    def across(k):
        other = me
        for bit in range(peers.bit_length()):
            size = 1 << bit
            if k & size:
                other = other + size - 2 * size * ((me // size) % 2)
        return other

    def swap_copy(k):
        return pltpu.make_async_remote_copy(
            src_ref=x_buf.at[0],
            dst_ref=x_buf.at[k],
            send_sem=x_send.at[k],
            recv_sem=x_recv.at[k],
            device_id=(ctx, across(k)),
            device_id_type=MESH,
        )

    barrier = pltpu.get_barrier_semaphore()
    for k in range(1, shards):
        pl.semaphore_signal(
            barrier, inc=1, device_id=((ctx + k) % shards, me), device_id_type=MESH
        )

    def greet(k, c):
        pl.semaphore_signal(
            barrier, inc=1, device_id=(ctx, (me + k) % peers), device_id_type=MESH
        )
        return c

    lax.fori_loop(1, peers, greet, 0)

    small = [
        pltpu.make_async_copy(hbm, inside, small_sem.at[i])
        for i, (hbm, inside) in enumerate(
            ((starts_hbm, starts_ref), (rate_hbm, rate_ref), (gain_hbm, gain_ref))
        )
    ]
    for copy in small:
        copy.start()

    def start_loads(pair):
        def go(h, c):
            for i in pair:
                load(i, h).start()
            return c
        lax.fori_loop(0, heads, go, 0)

    start_loads((0, 1))
    start_loads((2, 3))
    small[0].wait()

    row_at = lax.broadcasted_iota(jnp.int32, (CHUNK, CHUNK), 0)
    col_at = lax.broadcasted_iota(jnp.int32, (CHUNK, CHUNK), 1)
    lower = row_at >= col_at
    ones_low = jnp.where(lower, 1.0, 0.0).astype(BF16)
    for c in range(chunks):
        flags = starts_ref[:, c * CHUNK:(c + 1) * CHUNK].astype(F32)
        wide = jnp.broadcast_to(flags, (DH, CHUNK)).astype(BF16)
        run_row = dot(wide, ones_low, 1, 1)[0:1, :]
        run_col = dot(ones_low, wide, 1, 1)
        count = jnp.sum(flags, axis=1, keepdims=True)
        both = jnp.concatenate([run_col] * (CHUNK // DH), axis=1)
        joined[c] = jnp.where(lower & (both == run_row), 1.0, 0.0)
        in_mask[c] = jnp.where(run_col == 0.0, 1.0, 0.0)
        out_mask[c] = jnp.where(run_col == count, 1.0, 0.0)
        clear[c] = jnp.broadcast_to(jnp.where(count == 0.0, 1.0, 0.0), (8, DH))
    whole = jnp.sum(starts_ref[...].astype(F32), axis=1, keepdims=True)
    flags_buf[ctx] = jnp.broadcast_to(jnp.where(whole == 0.0, 1.0, 0.0), (8, DH))

    place = lax.broadcasted_iota(jnp.int32, (CHUNK, DH), 0).astype(F32)
    gap = jnp.maximum(row_at - col_at, 0).astype(F32)

    def reach_in(rate):
        return jnp.exp(-rate * (place + 1.0))

    def reach_out(rate):
        return jnp.exp(-rate * (CHUNK - 1.0 - place))

    def carry(rate, c):
        return clear[c] * jnp.exp(jnp.full((8, DH), -rate * CHUNK, F32))

    def spread(h, c):
        rate_rows[h] = jnp.full((8, DH), rate_ref[h], F32)
        return c

    def needs(which, late, step):
        at = shards - 1 - ctx if which else ctx
        size = size_of(late, step)
        upper = (at // size) % 2 == 1
        above = at // (2 * size)
        both = (above > 0) if late else (above < shards // (2 * size) - 1)
        return ~upper | both, upper | both

    def send_part(which, step, h, late):
        @pl.when(needs(which, late, step)[0])
        def _():
            scan_copy(which, step, h, late).start()

    table = {}

    def factor(which, first, last, use, other):
        kept = jnp.ones((8, DH), F32)
        for i in range(shards):
            flag = flags_buf[shards - 1 - i if which else i]
            kept = kept * jnp.where((i >= first) & (i < last), flag, 1.0)
        slot = sum(len(entry) for entry in table.values())
        kept_buf[slot] = jnp.where(use, kept, other)
        return slot, jnp.where(use, jnp.maximum(last - first, 0) * rows, 0).astype(F32)

    def make_table():
        for which in range(2):
            at = shards - 1 - ctx if which else ctx
            for late in (False, True):
                for step in range(steps):
                    size = size_of(late, step)
                    start = at - at % (2 * size)
                    middle, end, upper = start + size, start + 2 * size, at >= start + size
                    key = (which, late, step)
                    table[key] = []
                    if not late:
                        entries = [(middle, at, upper, 0.0), (middle, end, ~upper, 1.0), (middle, end, upper, 1.0)]
                    else:
                        size = size_of(late, min(step + 1, steps - 1))
                        begin = at - at % (2 * size)
                        half = begin + size
                        lower = at < half
                        first = (at - middle + start + 1, middle, upper, 0.0) if step == 0 else (start, middle, upper, 1.0)
                        entries = [first, (begin, half, lower, 1.0), (at + 1, half, lower, 0.0)]
                    for entry in entries[:1] if step == steps - 1 else entries:
                        table[key] = table[key] + [factor(which, *entry)]

    def put(which, h, late, state):
        own[which, 0, h] = state
        send_part(which, 0, h, late)

    def await_part(which, step, h, late):
        @pl.when(needs(which, late, step)[1])
        def _():
            scan_copy(which, step, h, late).wait_recv()

    def take(which, step, h, late, rate):
        needed = needs(which, late, step)[1]
        factors = [
            (kept_buf[slot] * jnp.exp(jnp.full((8, DH), -rate * length, F32)))[0:1, :]
            for slot, length in table[which, late, step]
        ]
        came = jnp.where(needed, got[which, step, h], 0.0)
        if not late:
            state = factors[0] * came
            if step > 0:
                state = state + pre[h]
        else:
            state = factors[0] * (came if step == 0 else pre[h])
            if step > 0:
                state = state + came
        if step == steps - 1:
            return state
        pre[h] = state
        own[which, step + 1, h] = (
            factors[1] * state + factors[2] * own[which, 0, h]
            if late
            else factors[1] * own[which, step, h] + factors[2] * came
        )
        send_part(which, step + 1, h, late)
        return None

    def take_pair(which, j):
        for step in range(steps - 1):
            for late in (False, True):
                await_part(which, step, 2 * j + int(late), late)
            for late in (False, True):
                h = 2 * j + int(late)
                take(which, step, h, late, rate_ref[h])

    def finish_pairs(which, work):
        def go(j, carried):
            for late in (False, True):
                await_part(which, steps - 1, 2 * j + int(late), late)
            for late in (False, True):
                work(2 * j + int(late), late)
            return carried
        lax.fori_loop(0, heads // 2, go, 0)

    def pairs(work, first=0):
        def go(j, carried):
            for late in (False, True):
                work(2 * j + int(late), late)
            return carried
        lax.fori_loop(first, heads // 2, go, 0)

    def part(c):
        return slice(c * CHUNK, (c + 1) * CHUNK)

    small[1].wait()
    small[2].wait()
    lax.fori_loop(0, heads, spread, 0)
    pl.semaphore_wait(barrier, shards + peers - 2)
    for k in range(1, shards):
        flag_copy(k).start()

    def make_states(h, late):
        load(0, h).wait()
        load(1, h).wait()
        rate = rate_ref[h]
        out = reach_out(rate)
        state = jnp.zeros((DH, DH), F32)
        for c in range(chunks):
            weighted = (ks[h, part(c), :].astype(F32) * (out * out_mask[c])).astype(BF16)
            add = dot(weighted, vs[h, part(c), :], 0, 0)
            d_state[h, c] = add
            keep = carry(rate, c)
            state = keep[0:1, :] * state + add
        put(0, h, late, state)

    pairs(make_states)
    sq_acc[...] = jnp.zeros_like(sq_acc)
    cr_acc[...] = jnp.zeros_like(cr_acc)
    for k in range(1, shards):
        flag_copy(k).wait_recv()
    make_table()

    def attend(h):
        load(2, h).wait()
        load(3, h).wait()
        decay = jnp.exp(-rate_ref[h] * gap)
        reach = reach_in(rate_ref[h])
        def raw(c):
            return dot(qs[h, part(c), :], ks[h, part(c), :], 1, 1)

        ready = [raw(c) for c in range(min(AHEAD, chunks))]
        for c in range(chunks):
            scores = ready.pop(0)
            if c + AHEAD < chunks:
                ready.append(raw(c + AHEAD))
            w = (scores * (decay * joined[c])).astype(BF16)
            weights[h, c] = jnp.transpose(w)
            att[h, part(c), :] = dot(w, vs[h, part(c), :], 1, 0)
            qw[h, part(c), :] = (qs[h, part(c), :].astype(F32) * (reach * in_mask[c])).astype(BF16)

    def attend_pair(j, carried):
        attend(2 * j)
        attend(2 * j + 1)
        take_pair(0, j)
        return carried

    lax.fori_loop(0, heads // 2, attend_pair, 0)

    def finish_attend(j, final):
        both = [(2 * j + int(late), late) for late in (False, True)]
        for h, late in both:
            await_part(0, steps - 1, h, late)
        states = [take(0, steps - 1, h, late, rate_ref[h]) for h, late in both]
        reaches = [reach_in(rate_ref[h]) for h, _ in both]
        for c in range(chunks):
            squares, crosses = sq_acc[part(c), :], cr_acc[part(c), :]
            for i, (h, _) in enumerate(both):
                small = states[i].astype(BF16)
                full_state[h, c] = small
                a = att[h, part(c), :] + (reaches[i] * in_mask[c]) * dot(qs[h, part(c), :], small, 1, 0)
                att[h, part(c), :] = a
                squares = squares + a * a
                crosses = crosses + gs[h, part(c), :].astype(F32) * gain_ref[pl.ds(h, 1), :] * a
                if c < chunks - 1:
                    states[i] = carry(rate_ref[h], c)[0:1, :] * states[i] + d_state[h, c]
            if final:
                x_buf[0, 0:1, part(c)] = jnp.sum(jnp.transpose(squares), axis=0, keepdims=True)
                x_buf[0, 1:2, part(c)] = jnp.sum(jnp.transpose(crosses), axis=0, keepdims=True)
            else:
                sq_acc[part(c), :] = squares
                cr_acc[part(c), :] = crosses

    def finish_early(j, carried):
        finish_attend(j, False)
        return carried

    lax.fori_loop(0, heads // 2 - 1, finish_early, 0)
    finish_attend(heads // 2 - 1, True)

    for k in reversed(range(1, peers)):
        swap_copy(k).start()
    sums = x_buf[0]
    for k in range(1, peers):
        swap_copy(k).wait_recv()
        sums = sums + x_buf[k]
    inverse = 1.0 / jnp.sqrt(sums[0:1, :] / total + EPSILON)
    coef = inverse * inverse * inverse * (sums[1:2, :] / total)
    inv_full[...] = jnp.transpose(jnp.broadcast_to(inverse, (DH, rows)))
    coef_full[...] = jnp.transpose(jnp.broadcast_to(coef, (DH, rows)))

    def make_grads(h, late):
        rate = rate_ref[h]
        gain = gain_ref[pl.ds(h, 1), :]
        state = jnp.zeros((DH, DH), F32)
        for c in reversed(range(chunks)):
            a, inv = att[h, part(c), :], inv_full[part(c), :]
            gained = gs[h, part(c), :].astype(F32) * gain
            grad = (inv * gained - a * coef_full[part(c), :]).astype(BF16)
            ga[h, part(c), :] = grad
            add = dot(qw[h, part(c), :], grad, 0, 0)
            d_grad[h, c] = add
            keep = carry(rate, c)
            state = keep[0:1, :] * state + add
        put(1, h, late, state)

    make_grads(0, False)
    make_grads(1, True)
    pairs(make_grads, 1)

    def inner_grads(h):
        rate = rate_ref[h]
        decay = jnp.exp(-rate * gap)
        reach = reach_in(rate)
        gain = gain_ref[pl.ds(h, 1), :]
        def raw(c):
            grad = ga[h, part(c), :]
            return dot(grad, vs[h, part(c), :], 1, 1), dot(grad, full_state[h, c], 1, 1)

        ready = [raw(c) for c in range(min(AHEAD_GRADS, chunks))]
        for c in range(chunks):
            wide, far = ready.pop(0)
            if c + AHEAD_GRADS < chunks:
                ready.append(raw(c + AHEAD_GRADS))
            n_out[part(c), cols(h)] = (att[h, part(c), :] * inv_full[part(c), :] * gain).astype(BF16)
            gvp[h, part(c), :] = dot(weights[h, c], ga[h, part(c), :], 1, 0)
            d = (wide * (decay * joined[c])).astype(BF16)
            gq = dot(d, ks[h, part(c), :], 1, 0) + (reach * in_mask[c]) * far
            gq_out[part(c), cols(h)] = gq.astype(BF16)
            gkp[h, part(c), :] = dot(d, qs[h, part(c), :], 0, 0)

    def inner_pair(j, carried):
        take_pair(1, j)
        inner_grads(2 * j)
        inner_grads(2 * j + 1)
        return carried

    lax.fori_loop(0, heads // 2, inner_pair, 0)

    def keep_last(h, late):
        last[h] = take(1, steps - 1, h, late, rate_ref[h])

    def drain(passes):
        def work(h, late):
            for which, step in passes:
                @pl.when(needs(which, late, step)[0])
                def _():
                    scan_copy(which, step, h, late).wait_send()
        pairs(work)

    drain([(0, step) for step in range(steps)] + [(1, step) for step in range(steps - 1)])
    for k in range(1, shards):
        flag_copy(k).wait_send()
    for k in range(1, peers):
        swap_copy(k).wait_send()
    finish_pairs(1, keep_last)
    drain([(1, steps - 1)])


def write_out(
    n_in, gq_in, gkp, gvp, ks, vs, d_grad, last, out_mask, clear, rate_rows,
    n_out, gq_out, gk_out, gv_out, gk, gv, sems, pair_sems,
):
    heads, rows, _ = ks.shape
    copies = [
        pltpu.make_async_copy(n_in, n_out, sems.at[0]),
        pltpu.make_async_copy(gq_in, gq_out, sems.at[1]),
    ]
    for copy in copies:
        copy.start()
    place = lax.broadcasted_iota(jnp.int32, (CHUNK, DH), 0).astype(F32)

    def pair_copies(j):
        width = gk.shape[1] // (heads // 2)
        cols = pl.ds(pl.multiple_of(j * width, width), width)
        return [
            pltpu.make_async_copy(gk.at[:, cols], gk_out.at[:, cols], pair_sems.at[0, j]),
            pltpu.make_async_copy(gv.at[:, cols], gv_out.at[:, cols], pair_sems.at[1, j]),
        ]

    def finish(h):
        cols = pl.ds(pl.multiple_of(h * DH, DH), DH)
        rate = rate_rows[h]
        out = jnp.exp(-rate[0:1, :] * (CHUNK - 1.0 - place))
        fade = jnp.exp(-rate * CHUNK)
        state = last[h]
        for c in reversed(range(rows // CHUNK)):
            part = slice(c * CHUNK, (c + 1) * CHUNK)
            small = state.astype(BF16)
            reach = out * out_mask[c]
            gk[part, cols] = (gkp[h, part, :] + reach * dot(vs[h, part, :], small, 1, 1)).astype(BF16)
            gv[part, cols] = (gvp[h, part, :] + reach * dot(ks[h, part, :], small, 1, 0)).astype(BF16)
            if c > 0:
                state = (clear[c] * fade)[0:1, :] * state + d_grad[h, c]

    def go(j, carried):
        finish(2 * j)
        finish(2 * j + 1)
        for copy in pair_copies(j):
            copy.start()
        return carried

    lax.fori_loop(0, heads // 2, go, 0)

    def drain(j, carried):
        for copy in pair_copies(j):
            copy.wait()
        return carried

    lax.fori_loop(0, heads // 2, drain, 0)
    for copy in copies:
        copy.wait()


def body(shards, peers, query_rows, key_rows, value_rows, decay_rate, starts, norm_gain, grad_out):
    rows, features = query_rows.shape
    heads = features // DH
    chunks = rows // CHUNK
    steps = (shards - 1).bit_length()
    big = jax.ShapeDtypeStruct((rows, features), BF16)
    whole = pl.BlockSpec(memory_space=pltpu.HBM)
    inside = pl.BlockSpec(memory_space=pltpu.VMEM)

    def head_rows(dtype):
        return pltpu.VMEM((heads, rows, DH), dtype)

    dma = pltpu.SemaphoreType.DMA
    handed = (
        (pltpu.VMEM((rows, features), BF16),) * 2
        + (head_rows(F32),) * 2
        + (head_rows(BF16),) * 2
        + (
            pltpu.VMEM((heads, chunks, DH, DH), F32),
            pltpu.VMEM((heads, DH, DH), F32),
            pltpu.VMEM((chunks, CHUNK, DH), F32),
            pltpu.VMEM((chunks, 8, DH), F32),
            pltpu.VMEM((heads, 8, DH), F32),
        )
    )
    kept = pl.pallas_call(
        functools.partial(kernel, shards, steps, peers, HEADS * DH),
        out_shape=handed,
        in_specs=[whole] * 7,
        out_specs=(inside,) * len(handed),
        scratch_shapes=[
            pltpu.SMEM((heads,), F32),
            pltpu.VMEM((1, rows), jnp.int32),
            pltpu.VMEM((heads, DH), F32),
        ]
        + [head_rows(BF16)] * 3
        + [head_rows(F32), head_rows(BF16), pltpu.VMEM((heads, chunks, CHUNK, CHUNK), BF16)]
        + [
            pltpu.VMEM((chunks, CHUNK, CHUNK), F32),
            pltpu.VMEM((chunks, CHUNK, DH), F32),
            pltpu.VMEM((heads, chunks, DH, DH), F32),
            pltpu.VMEM((heads, chunks, DH, DH), BF16),
            pltpu.VMEM((2, steps, heads, DH, DH), F32),
            pltpu.VMEM((2, steps, heads, DH, DH), F32),
            pltpu.VMEM((heads, DH, DH), F32),
            pltpu.VMEM((shards, 8, DH), F32),
            pltpu.VMEM((12 * steps, 8, DH), F32),
            pltpu.VMEM((rows, DH), F32),
            pltpu.VMEM((rows, DH), F32),
            pltpu.VMEM((rows, DH), F32),
            pltpu.VMEM((rows, DH), F32),
            pltpu.VMEM((peers, 2, rows), F32),
            dma((3,)),
            dma((4, heads)),
            dma((2, steps, heads)),
            dma((2, steps, heads)),
            dma((shards,)),
            dma((shards,)),
            dma((peers,)),
            dma((peers,)),
        ],
        compiler_params=pltpu.CompilerParams(
            collective_id=0, has_side_effects=True, vmem_limit_bytes=34 * 1024 * 1024
        ),
    )(
        query_rows, key_rows, value_rows, grad_out, decay_rate,
        starts.reshape(1, rows), norm_gain.reshape(heads, DH),
    )
    return pl.pallas_call(
        write_out,
        out_shape=(big,) * 4,
        in_specs=[inside] * len(handed),
        out_specs=(whole,) * 4,
        scratch_shapes=[
            pltpu.VMEM((rows, features), BF16),
            pltpu.VMEM((rows, features), BF16),
            dma((2,)),
            dma((2, heads // 2)),
        ],
        compiler_params=pltpu.CompilerParams(vmem_limit_bytes=6 * 1024 * 1024),
    )(*kept)


def solution(mesh):
    both = P("ctx", "head")
    return jax.shard_map(
        functools.partial(body, mesh.shape["ctx"], mesh.shape["head"]),
        mesh=mesh,
        in_specs=(both, both, both, P("head"), P("ctx"), P("head"), both),
        out_specs=(both,) * 4,
        check_vma=False,
    )
```

```python
import functools

import jax
import jax.numpy as jnp
from jax import lax
from jax.experimental import pallas as pl
from jax.experimental.pallas import tpu as pltpu
from jax.sharding import PartitionSpec as P

HEADS = 64
DH = 128
CHUNK = 128
AHEAD = 2
AHEAD_GRADS = 3
EPSILON = 1e-06
MESH = pl.DeviceIdType.MESH
F32 = jnp.float32
BF16 = jnp.bfloat16


def dot(a, b, da, db):
    return lax.dot_general(a, b, (((da,), (db,)), ((), ())), preferred_element_type=F32)


def kernel(
    shards, steps, peers, total,
    q_hbm, k_hbm, v_hbm, g_hbm, rate_hbm, starts_hbm, gain_hbm,
    n_out, gq_out, gkp, gvp, ks, vs, d_grad, last, out_mask, clear, rate_rows,
    rate_ref, starts_ref, gain_ref,
    qs, gs, qw, gained, att, ga, weights,
    joined, in_mask, d_state, full_state,
    own, got, pre, flags_buf, kept_buf, sq_acc, cr_acc, inv_full, coef_full, x_buf,
    small_sem, in_sem, s_send, s_recv, f_send, f_recv, x_send, x_recv,
):
    heads, rows, _ = qs.shape
    chunks = rows // CHUNK
    ctx = lax.axis_index("ctx")
    me = lax.axis_index("head")

    def cols(h):
        return pl.ds(pl.multiple_of(h * DH, DH), DH)

    def load(i, h):
        hbm, buf = ((k_hbm, ks), (v_hbm, vs), (q_hbm, qs), (g_hbm, gs))[i]
        return pltpu.make_async_copy(hbm.at[:, cols(h)], buf.at[h], in_sem.at[i, h])

    def size_of(late, step):
        return 1 << (steps - 1 - step if late else step)

    def scan_copy(which, step, h, late):
        size = size_of(late, step)
        return pltpu.make_async_remote_copy(
            src_ref=own.at[which, step, h],
            dst_ref=got.at[which, step, h],
            send_sem=s_send.at[which, step, h],
            recv_sem=s_recv.at[which, step, h],
            device_id=(ctx + size - 2 * size * ((ctx // size) % 2), me),
            device_id_type=MESH,
        )

    def flag_copy(k):
        return pltpu.make_async_remote_copy(
            src_ref=flags_buf.at[ctx],
            dst_ref=flags_buf.at[ctx],
            send_sem=f_send.at[k],
            recv_sem=f_recv.at[k],
            device_id=((ctx + k) % shards, me),
            device_id_type=MESH,
        )

    def across(k):
        other = me
        for bit in range(peers.bit_length()):
            size = 1 << bit
            if k & size:
                other = other + size - 2 * size * ((me // size) % 2)
        return other

    def swap_copy(k):
        return pltpu.make_async_remote_copy(
            src_ref=x_buf.at[0],
            dst_ref=x_buf.at[k],
            send_sem=x_send.at[k],
            recv_sem=x_recv.at[k],
            device_id=(ctx, across(k)),
            device_id_type=MESH,
        )

    barrier = pltpu.get_barrier_semaphore()
    for k in range(1, shards):
        pl.semaphore_signal(
            barrier, inc=1, device_id=((ctx + k) % shards, me), device_id_type=MESH
        )

    def greet(k, c):
        pl.semaphore_signal(
            barrier, inc=1, device_id=(ctx, (me + k) % peers), device_id_type=MESH
        )
        return c

    lax.fori_loop(1, peers, greet, 0)

    small = [
        pltpu.make_async_copy(hbm, inside, small_sem.at[i])
        for i, (hbm, inside) in enumerate(
            ((starts_hbm, starts_ref), (rate_hbm, rate_ref), (gain_hbm, gain_ref))
        )
    ]
    for copy in small:
        copy.start()

    def start_loads(pair):
        def go(h, c):
            for i in pair:
                load(i, h).start()
            return c
        lax.fori_loop(0, heads, go, 0)

    start_loads((0, 1))
    start_loads((2, 3))
    small[0].wait()

    row_at = lax.broadcasted_iota(jnp.int32, (CHUNK, CHUNK), 0)
    col_at = lax.broadcasted_iota(jnp.int32, (CHUNK, CHUNK), 1)
    lower = row_at >= col_at
    ones_low = jnp.where(lower, 1.0, 0.0).astype(BF16)
    for c in range(chunks):
        flags = starts_ref[:, c * CHUNK:(c + 1) * CHUNK].astype(F32)
        wide = jnp.broadcast_to(flags, (DH, CHUNK)).astype(BF16)
        run_row = dot(wide, ones_low, 1, 1)[0:1, :]
        run_col = dot(ones_low, wide, 1, 1)
        count = jnp.sum(flags, axis=1, keepdims=True)
        both = jnp.concatenate([run_col] * (CHUNK // DH), axis=1)
        joined[c] = jnp.where(lower & (both == run_row), 1.0, 0.0)
        in_mask[c] = jnp.where(run_col == 0.0, 1.0, 0.0)
        out_mask[c] = jnp.where(run_col == count, 1.0, 0.0)
        clear[c] = jnp.broadcast_to(jnp.where(count == 0.0, 1.0, 0.0), (8, DH))
    whole = jnp.sum(starts_ref[...].astype(F32), axis=1, keepdims=True)
    flags_buf[ctx] = jnp.broadcast_to(jnp.where(whole == 0.0, 1.0, 0.0), (8, DH))

    place = lax.broadcasted_iota(jnp.int32, (CHUNK, DH), 0).astype(F32)
    gap = jnp.maximum(row_at - col_at, 0).astype(F32)

    def reach_in(rate):
        return jnp.exp(-rate * (place + 1.0))

    def reach_out(rate):
        return jnp.exp(-rate * (CHUNK - 1.0 - place))

    def carry(rate, c):
        return clear[c] * jnp.exp(jnp.full((8, DH), -rate * CHUNK, F32))

    def spread(h, c):
        rate_rows[h] = jnp.full((8, DH), rate_ref[h], F32)
        return c

    def needs(which, late, step):
        at = shards - 1 - ctx if which else ctx
        size = size_of(late, step)
        upper = (at // size) % 2 == 1
        above = at // (2 * size)
        both = (above > 0) if late else (above < shards // (2 * size) - 1)
        return ~upper | both, upper | both

    def send_part(which, step, h, late):
        @pl.when(needs(which, late, step)[0])
        def _():
            scan_copy(which, step, h, late).start()

    table = {}

    def factor(which, first, last, use, other):
        kept = jnp.ones((8, DH), F32)
        for i in range(shards):
            flag = flags_buf[shards - 1 - i if which else i]
            kept = kept * jnp.where((i >= first) & (i < last), flag, 1.0)
        slot = sum(len(entry) for entry in table.values())
        kept_buf[slot] = jnp.where(use, kept, other)
        return slot, jnp.where(use, jnp.maximum(last - first, 0) * rows, 0).astype(F32)

    def make_table():
        for which in range(2):
            at = shards - 1 - ctx if which else ctx
            for late in (False, True):
                for step in range(steps):
                    size = size_of(late, step)
                    start = at - at % (2 * size)
                    middle, end, upper = start + size, start + 2 * size, at >= start + size
                    key = (which, late, step)
                    table[key] = []
                    if not late:
                        entries = [(middle, at, upper, 0.0), (middle, end, ~upper, 1.0), (middle, end, upper, 1.0)]
                    else:
                        size = size_of(late, min(step + 1, steps - 1))
                        begin = at - at % (2 * size)
                        half = begin + size
                        lower = at < half
                        first = (at - middle + start + 1, middle, upper, 0.0) if step == 0 else (start, middle, upper, 1.0)
                        entries = [first, (begin, half, lower, 1.0), (at + 1, half, lower, 0.0)]
                    for entry in entries[:1] if step == steps - 1 else entries:
                        table[key] = table[key] + [factor(which, *entry)]

    def put(which, h, late, state):
        own[which, 0, h] = state
        send_part(which, 0, h, late)

    def await_part(which, step, h, late):
        @pl.when(needs(which, late, step)[1])
        def _():
            scan_copy(which, step, h, late).wait_recv()

    def take(which, step, h, late, rate):
        needed = needs(which, late, step)[1]
        factors = [
            (kept_buf[slot] * jnp.exp(jnp.full((8, DH), -rate * length, F32)))[0:1, :]
            for slot, length in table[which, late, step]
        ]
        came = jnp.where(needed, got[which, step, h], 0.0)
        if not late:
            state = factors[0] * came
            if step > 0:
                state = state + pre[h]
        else:
            state = factors[0] * (came if step == 0 else pre[h])
            if step > 0:
                state = state + came
        if step == steps - 1:
            return state
        pre[h] = state
        own[which, step + 1, h] = (
            factors[1] * state + factors[2] * own[which, 0, h]
            if late
            else factors[1] * own[which, step, h] + factors[2] * came
        )
        send_part(which, step + 1, h, late)
        return None

    def take_pair(which, j):
        for step in range(steps - 1):
            for late in (False, True):
                await_part(which, step, 2 * j + int(late), late)
            for late in (False, True):
                h = 2 * j + int(late)
                take(which, step, h, late, rate_ref[h])

    def finish_pairs(which, work):
        def go(j, carried):
            for late in (False, True):
                await_part(which, steps - 1, 2 * j + int(late), late)
            for late in (False, True):
                work(2 * j + int(late), late)
            return carried
        lax.fori_loop(0, heads // 2, go, 0)

    def pairs(work, first=0):
        def go(j, carried):
            for late in (False, True):
                work(2 * j + int(late), late)
            return carried
        lax.fori_loop(first, heads // 2, go, 0)

    def part(c):
        return slice(c * CHUNK, (c + 1) * CHUNK)

    small[1].wait()
    small[2].wait()
    lax.fori_loop(0, heads, spread, 0)
    pl.semaphore_wait(barrier, shards + peers - 2)
    for k in range(1, shards):
        flag_copy(k).start()

    def make_states(h, late):
        load(0, h).wait()
        load(1, h).wait()
        rate = rate_ref[h]
        out = reach_out(rate)
        state = jnp.zeros((DH, DH), F32)
        for c in range(chunks):
            weighted = (ks[h, part(c), :].astype(F32) * (out * out_mask[c])).astype(BF16)
            add = dot(weighted, vs[h, part(c), :], 0, 0)
            d_state[h, c] = add
            keep = carry(rate, c)
            state = keep[0:1, :] * state + add
        put(0, h, late, state)

    pairs(make_states)
    sq_acc[...] = jnp.zeros_like(sq_acc)
    cr_acc[...] = jnp.zeros_like(cr_acc)
    for k in range(1, shards):
        flag_copy(k).wait_recv()
    make_table()

    def attend(h):
        load(2, h).wait()
        load(3, h).wait()
        decay = jnp.exp(-rate_ref[h] * gap)
        reach = reach_in(rate_ref[h])
        def raw(c):
            return dot(qs[h, part(c), :], ks[h, part(c), :], 1, 1)

        ready = [raw(c) for c in range(min(AHEAD, chunks))]
        for c in range(chunks):
            scores = ready.pop(0)
            if c + AHEAD < chunks:
                ready.append(raw(c + AHEAD))
            w = (scores * (decay * joined[c])).astype(BF16)
            weights[h, c] = jnp.transpose(w)
            att[h, part(c), :] = dot(w, vs[h, part(c), :], 1, 0)
            near = (qs[h, part(c), :].astype(F32) * (reach * in_mask[c])).astype(BF16)
            qw[h, c] = jnp.transpose(near)
            gained[h, part(c), :] = gs[h, part(c), :].astype(F32) * gain_ref[pl.ds(h, 1), :]

    def attend_pair(j, carried):
        attend(2 * j)
        attend(2 * j + 1)
        take_pair(0, j)
        return carried

    lax.fori_loop(0, heads // 2, attend_pair, 0)

    def finish_attend(j, final):
        both = [(2 * j + int(late), late) for late in (False, True)]
        for h, late in both:
            await_part(0, steps - 1, h, late)
        states = [take(0, steps - 1, h, late, rate_ref[h]) for h, late in both]
        reaches = [reach_in(rate_ref[h]) for h, _ in both]
        for c in range(chunks):
            squares, crosses = sq_acc[part(c), :], cr_acc[part(c), :]
            for i, (h, _) in enumerate(both):
                small = states[i].astype(BF16)
                full_state[h, c] = small
                a = att[h, part(c), :] + (reaches[i] * in_mask[c]) * dot(qs[h, part(c), :], small, 1, 0)
                att[h, part(c), :] = a
                squares = squares + a * a
                crosses = crosses + gained[h, part(c), :] * a
                if c < chunks - 1:
                    states[i] = carry(rate_ref[h], c)[0:1, :] * states[i] + d_state[h, c]
            if final:
                x_buf[0, 0:1, part(c)] = jnp.sum(jnp.transpose(squares), axis=0, keepdims=True)
                x_buf[0, 1:2, part(c)] = jnp.sum(jnp.transpose(crosses), axis=0, keepdims=True)
            else:
                sq_acc[part(c), :] = squares
                cr_acc[part(c), :] = crosses

    def finish_early(j, carried):
        finish_attend(j, False)
        return carried

    lax.fori_loop(0, heads // 2 - 1, finish_early, 0)
    finish_attend(heads // 2 - 1, True)

    for k in reversed(range(1, peers)):
        swap_copy(k).start()
    sums = x_buf[0]
    for k in range(1, peers):
        swap_copy(k).wait_recv()
        sums = sums + x_buf[k]
    inverse = 1.0 / jnp.sqrt(sums[0:1, :] / total + EPSILON)
    coef = inverse * inverse * inverse * (sums[1:2, :] / total)
    inv_full[...] = jnp.transpose(jnp.broadcast_to(inverse, (DH, rows)))
    coef_full[...] = jnp.transpose(jnp.broadcast_to(coef, (DH, rows)))

    def make_grads(h, late):
        rate = rate_ref[h]
        state = jnp.zeros((DH, DH), F32)
        for c in reversed(range(chunks)):
            a, inv = att[h, part(c), :], inv_full[part(c), :]
            grad = (inv * gained[h, part(c), :] - a * coef_full[part(c), :]).astype(BF16)
            ga[h, part(c), :] = grad
            add = dot(qw[h, c], grad, 1, 0)
            d_grad[h, c] = add
            keep = carry(rate, c)
            state = keep[0:1, :] * state + add
        put(1, h, late, state)

    make_grads(0, False)
    make_grads(1, True)
    pairs(make_grads, 1)

    def inner_grads(h):
        rate = rate_ref[h]
        decay = jnp.exp(-rate * gap)
        reach = reach_in(rate)
        gain = gain_ref[pl.ds(h, 1), :]
        def raw(c):
            grad = ga[h, part(c), :]
            return dot(grad, vs[h, part(c), :], 1, 1), dot(grad, full_state[h, c], 1, 1)

        ready = [raw(c) for c in range(min(AHEAD_GRADS, chunks))]
        for c in range(chunks):
            wide, far = ready.pop(0)
            if c + AHEAD_GRADS < chunks:
                ready.append(raw(c + AHEAD_GRADS))
            n_out[part(c), cols(h)] = (att[h, part(c), :] * inv_full[part(c), :] * gain).astype(BF16)
            gvp[h, part(c), :] = dot(weights[h, c], ga[h, part(c), :], 1, 0)
            d = (wide * (decay * joined[c])).astype(BF16)
            gq = dot(d, ks[h, part(c), :], 1, 0) + (reach * in_mask[c]) * far
            gq_out[part(c), cols(h)] = gq.astype(BF16)
            gkp[h, part(c), :] = dot(d, qs[h, part(c), :], 0, 0)

    def inner_pair(j, carried):
        take_pair(1, j)
        inner_grads(2 * j)
        inner_grads(2 * j + 1)
        return carried

    lax.fori_loop(0, heads // 2, inner_pair, 0)

    def keep_last(h, late):
        last[h] = take(1, steps - 1, h, late, rate_ref[h])

    def drain(passes):
        def work(h, late):
            for which, step in passes:
                @pl.when(needs(which, late, step)[0])
                def _():
                    scan_copy(which, step, h, late).wait_send()
        pairs(work)

    drain([(0, step) for step in range(steps)] + [(1, step) for step in range(steps - 1)])
    for k in range(1, shards):
        flag_copy(k).wait_send()
    for k in range(1, peers):
        swap_copy(k).wait_send()
    finish_pairs(1, keep_last)
    drain([(1, steps - 1)])


def write_out(
    n_in, gq_in, gkp, gvp, ks, vs, d_grad, last, out_mask, clear, rate_rows,
    n_out, gq_out, gk_out, gv_out, gk, gv, sems, pair_sems,
):
    heads, rows, _ = ks.shape
    copies = [
        pltpu.make_async_copy(n_in, n_out, sems.at[0]),
        pltpu.make_async_copy(gq_in, gq_out, sems.at[1]),
    ]
    for copy in copies:
        copy.start()
    place = lax.broadcasted_iota(jnp.int32, (CHUNK, DH), 0).astype(F32)

    def pair_copies(j):
        width = gk.shape[1] // (heads // 2)
        cols = pl.ds(pl.multiple_of(j * width, width), width)
        return [
            pltpu.make_async_copy(gk.at[:, cols], gk_out.at[:, cols], pair_sems.at[0, j]),
            pltpu.make_async_copy(gv.at[:, cols], gv_out.at[:, cols], pair_sems.at[1, j]),
        ]

    def finish(h):
        cols = pl.ds(pl.multiple_of(h * DH, DH), DH)
        rate = rate_rows[h]
        out = jnp.exp(-rate[0:1, :] * (CHUNK - 1.0 - place))
        fade = jnp.exp(-rate * CHUNK)
        state = last[h]
        for c in reversed(range(rows // CHUNK)):
            part = slice(c * CHUNK, (c + 1) * CHUNK)
            small = state.astype(BF16)
            reach = out * out_mask[c]
            gk[part, cols] = (gkp[h, part, :] + reach * dot(vs[h, part, :], small, 1, 1)).astype(BF16)
            gv[part, cols] = (gvp[h, part, :] + reach * dot(ks[h, part, :], small, 1, 0)).astype(BF16)
            if c > 0:
                state = (clear[c] * fade)[0:1, :] * state + d_grad[h, c]

    def go(j, carried):
        finish(2 * j)
        finish(2 * j + 1)
        for copy in pair_copies(j):
            copy.start()
        return carried

    lax.fori_loop(0, heads // 2, go, 0)

    def drain(j, carried):
        for copy in pair_copies(j):
            copy.wait()
        return carried

    lax.fori_loop(0, heads // 2, drain, 0)
    for copy in copies:
        copy.wait()


def body(shards, peers, query_rows, key_rows, value_rows, decay_rate, starts, norm_gain, grad_out):
    rows, features = query_rows.shape
    heads = features // DH
    chunks = rows // CHUNK
    steps = (shards - 1).bit_length()
    big = jax.ShapeDtypeStruct((rows, features), BF16)
    whole = pl.BlockSpec(memory_space=pltpu.HBM)
    inside = pl.BlockSpec(memory_space=pltpu.VMEM)

    def head_rows(dtype):
        return pltpu.VMEM((heads, rows, DH), dtype)

    dma = pltpu.SemaphoreType.DMA
    handed = (
        (pltpu.VMEM((rows, features), BF16),) * 2
        + (head_rows(F32),) * 2
        + (head_rows(BF16),) * 2
        + (
            pltpu.VMEM((heads, chunks, DH, DH), F32),
            pltpu.VMEM((heads, DH, DH), F32),
            pltpu.VMEM((chunks, CHUNK, DH), F32),
            pltpu.VMEM((chunks, 8, DH), F32),
            pltpu.VMEM((heads, 8, DH), F32),
        )
    )
    kept = pl.pallas_call(
        functools.partial(kernel, shards, steps, peers, HEADS * DH),
        out_shape=handed,
        in_specs=[whole] * 7,
        out_specs=(inside,) * len(handed),
        scratch_shapes=[
            pltpu.SMEM((heads,), F32),
            pltpu.VMEM((1, rows), jnp.int32),
            pltpu.VMEM((heads, DH), F32),
        ]
        + [head_rows(BF16)] * 2
        + [pltpu.VMEM((heads, chunks, DH, CHUNK), BF16), head_rows(F32)]
        + [head_rows(F32), head_rows(BF16), pltpu.VMEM((heads, chunks, CHUNK, CHUNK), BF16)]
        + [
            pltpu.VMEM((chunks, CHUNK, CHUNK), F32),
            pltpu.VMEM((chunks, CHUNK, DH), F32),
            pltpu.VMEM((heads, chunks, DH, DH), F32),
            pltpu.VMEM((heads, chunks, DH, DH), BF16),
            pltpu.VMEM((2, steps, heads, DH, DH), F32),
            pltpu.VMEM((2, steps, heads, DH, DH), F32),
            pltpu.VMEM((heads, DH, DH), F32),
            pltpu.VMEM((shards, 8, DH), F32),
            pltpu.VMEM((12 * steps, 8, DH), F32),
            pltpu.VMEM((rows, DH), F32),
            pltpu.VMEM((rows, DH), F32),
            pltpu.VMEM((rows, DH), F32),
            pltpu.VMEM((rows, DH), F32),
            pltpu.VMEM((peers, 2, rows), F32),
            dma((3,)),
            dma((4, heads)),
            dma((2, steps, heads)),
            dma((2, steps, heads)),
            dma((shards,)),
            dma((shards,)),
            dma((peers,)),
            dma((peers,)),
        ],
        compiler_params=pltpu.CompilerParams(
            collective_id=0, has_side_effects=True, vmem_limit_bytes=34 * 1024 * 1024
        ),
    )(
        query_rows, key_rows, value_rows, grad_out, decay_rate,
        starts.reshape(1, rows), norm_gain.reshape(heads, DH),
    )
    return pl.pallas_call(
        write_out,
        out_shape=(big,) * 4,
        in_specs=[inside] * len(handed),
        out_specs=(whole,) * 4,
        scratch_shapes=[
            pltpu.VMEM((rows, features), BF16),
            pltpu.VMEM((rows, features), BF16),
            dma((2,)),
            dma((2, heads // 2)),
        ],
        compiler_params=pltpu.CompilerParams(vmem_limit_bytes=6 * 1024 * 1024),
    )(*kept)


def solution(mesh):
    both = P("ctx", "head")
    return jax.shard_map(
        functools.partial(body, mesh.shape["ctx"], mesh.shape["head"]),
        mesh=mesh,
        in_specs=(both, both, both, P("head"), P("ctx"), P("head"), both),
        out_specs=(both,) * 4,
        check_vma=False,
    )
```

```python
import functools

import jax
import jax.numpy as jnp
from jax import lax
from jax.experimental import pallas as pl
from jax.experimental.pallas import tpu as pltpu
from jax.sharding import PartitionSpec as P

HEADS = 64
DH = 128
CHUNK = 128
AHEAD = 2
AHEAD_GRADS = 3
EPSILON = 1e-06
MESH = pl.DeviceIdType.MESH
F32 = jnp.float32
BF16 = jnp.bfloat16


def dot(a, b, da, db):
    return lax.dot_general(a, b, (((da,), (db,)), ((), ())), preferred_element_type=F32)


def kernel(
    shards, steps, peers, total,
    q_hbm, k_hbm, v_hbm, g_hbm, rate_hbm, starts_hbm, gain_hbm,
    n_out, gq_out, gkp, gvp, ks, vs, d_grad, last, out_mask, clear, rate_rows,
    rate_ref, starts_ref, gain_ref,
    qs, gs, qw, gained, att, ga, weights,
    joined, in_mask, d_state, full_state,
    own, got, pre, flags_buf, kept_buf, sq_acc, cr_acc, inv_full, coef_full, x_buf,
    small_sem, in_sem, s_send, s_recv, f_send, f_recv, x_send, x_recv,
):
    heads, rows, _ = qs.shape
    chunks = rows // CHUNK
    ctx = lax.axis_index("ctx")
    me = lax.axis_index("head")

    def cols(h):
        return pl.ds(pl.multiple_of(h * DH, DH), DH)

    def load(i, h):
        hbm, buf = ((k_hbm, ks), (v_hbm, vs), (q_hbm, qs), (g_hbm, gs))[i]
        return pltpu.make_async_copy(hbm.at[:, cols(h)], buf.at[h], in_sem.at[i, h])

    def size_of(late, step):
        return 1 << (steps - 1 - step if late else step)

    def scan_copy(which, step, h, late):
        size = size_of(late, step)
        return pltpu.make_async_remote_copy(
            src_ref=own.at[which, step, h],
            dst_ref=got.at[which, step, h],
            send_sem=s_send.at[which, step, h],
            recv_sem=s_recv.at[which, step, h],
            device_id=(ctx + size - 2 * size * ((ctx // size) % 2), me),
            device_id_type=MESH,
        )

    def flag_copy(k):
        return pltpu.make_async_remote_copy(
            src_ref=flags_buf.at[ctx],
            dst_ref=flags_buf.at[ctx],
            send_sem=f_send.at[k],
            recv_sem=f_recv.at[k],
            device_id=((ctx + k) % shards, me),
            device_id_type=MESH,
        )

    def across(k):
        other = me
        for bit in range(peers.bit_length()):
            size = 1 << bit
            if k & size:
                other = other + size - 2 * size * ((me // size) % 2)
        return other

    def swap_copy(k):
        return pltpu.make_async_remote_copy(
            src_ref=x_buf.at[0],
            dst_ref=x_buf.at[k],
            send_sem=x_send.at[k],
            recv_sem=x_recv.at[k],
            device_id=(ctx, across(k)),
            device_id_type=MESH,
        )

    barrier = pltpu.get_barrier_semaphore()
    for k in range(1, shards):
        pl.semaphore_signal(
            barrier, inc=1, device_id=((ctx + k) % shards, me), device_id_type=MESH
        )

    def greet(k, c):
        pl.semaphore_signal(
            barrier, inc=1, device_id=(ctx, (me + k) % peers), device_id_type=MESH
        )
        return c

    lax.fori_loop(1, peers, greet, 0)

    small = [
        pltpu.make_async_copy(hbm, inside, small_sem.at[i])
        for i, (hbm, inside) in enumerate(
            ((starts_hbm, starts_ref), (rate_hbm, rate_ref), (gain_hbm, gain_ref))
        )
    ]
    for copy in small:
        copy.start()

    def start_loads(pair, first, last):
        def go(h, c):
            for i in pair:
                load(i, h).start()
            return c
        lax.fori_loop(first, last, go, 0)

    start_loads((0, 1), 0, 2)
    small[0].wait()

    row_at = lax.broadcasted_iota(jnp.int32, (CHUNK, CHUNK), 0)
    col_at = lax.broadcasted_iota(jnp.int32, (CHUNK, CHUNK), 1)
    lower = row_at >= col_at
    ones_low = jnp.where(lower, 1.0, 0.0).astype(BF16)
    for c in range(chunks):
        flags = starts_ref[:, c * CHUNK:(c + 1) * CHUNK].astype(F32)
        wide = jnp.broadcast_to(flags, (DH, CHUNK)).astype(BF16)
        run_row = dot(wide, ones_low, 1, 1)[0:1, :]
        run_col = dot(ones_low, wide, 1, 1)
        count = jnp.sum(flags, axis=1, keepdims=True)
        both = jnp.concatenate([run_col] * (CHUNK // DH), axis=1)
        joined[c] = jnp.where(lower & (both == run_row), 1.0, 0.0)
        in_mask[c] = jnp.where(run_col == 0.0, 1.0, 0.0)
        out_mask[c] = jnp.where(run_col == count, 1.0, 0.0)
        clear[c] = jnp.broadcast_to(jnp.where(count == 0.0, 1.0, 0.0), (8, DH))
    whole = jnp.sum(starts_ref[...].astype(F32), axis=1, keepdims=True)
    flags_buf[ctx] = jnp.broadcast_to(jnp.where(whole == 0.0, 1.0, 0.0), (8, DH))

    place = lax.broadcasted_iota(jnp.int32, (CHUNK, DH), 0).astype(F32)
    gap = jnp.maximum(row_at - col_at, 0).astype(F32)

    def reach_in(rate):
        return jnp.exp(-rate * (place + 1.0))

    def reach_out(rate):
        return jnp.exp(-rate * (CHUNK - 1.0 - place))

    def carry(rate, c):
        return clear[c] * jnp.exp(jnp.full((8, DH), -rate * CHUNK, F32))

    def spread(h, c):
        rate_rows[h] = jnp.full((8, DH), rate_ref[h], F32)
        return c

    def needs(which, late, step):
        at = shards - 1 - ctx if which else ctx
        size = size_of(late, step)
        upper = (at // size) % 2 == 1
        above = at // (2 * size)
        both = (above > 0) if late else (above < shards // (2 * size) - 1)
        return ~upper | both, upper | both

    def send_part(which, step, h, late):
        @pl.when(needs(which, late, step)[0])
        def _():
            scan_copy(which, step, h, late).start()

    table = {}

    def factor(which, first, last, use, other):
        kept = jnp.ones((8, DH), F32)
        for i in range(shards):
            flag = flags_buf[shards - 1 - i if which else i]
            kept = kept * jnp.where((i >= first) & (i < last), flag, 1.0)
        slot = sum(len(entry) for entry in table.values())
        kept_buf[slot] = jnp.where(use, kept, other)
        return slot, jnp.where(use, jnp.maximum(last - first, 0) * rows, 0).astype(F32)

    def make_table():
        for which in range(2):
            at = shards - 1 - ctx if which else ctx
            for late in (False, True):
                for step in range(steps):
                    size = size_of(late, step)
                    start = at - at % (2 * size)
                    middle, end, upper = start + size, start + 2 * size, at >= start + size
                    key = (which, late, step)
                    table[key] = []
                    if not late:
                        entries = [(middle, at, upper, 0.0), (middle, end, ~upper, 1.0), (middle, end, upper, 1.0)]
                    else:
                        size = size_of(late, min(step + 1, steps - 1))
                        begin = at - at % (2 * size)
                        half = begin + size
                        lower = at < half
                        first = (at - middle + start + 1, middle, upper, 0.0) if step == 0 else (start, middle, upper, 1.0)
                        entries = [first, (begin, half, lower, 1.0), (at + 1, half, lower, 0.0)]
                    for entry in entries[:1] if step == steps - 1 else entries:
                        table[key] = table[key] + [factor(which, *entry)]

    def put(which, h, late, state):
        own[which, 0, h] = state
        send_part(which, 0, h, late)

    def await_part(which, step, h, late):
        @pl.when(needs(which, late, step)[1])
        def _():
            scan_copy(which, step, h, late).wait_recv()

    def take(which, step, h, late, rate):
        needed = needs(which, late, step)[1]
        factors = [
            (kept_buf[slot] * jnp.exp(jnp.full((8, DH), -rate * length, F32)))[0:1, :]
            for slot, length in table[which, late, step]
        ]
        came = jnp.where(needed, got[which, step, h], 0.0)
        if not late:
            state = factors[0] * came
            if step > 0:
                state = state + pre[h]
        else:
            state = factors[0] * (came if step == 0 else pre[h])
            if step > 0:
                state = state + came
        if step == steps - 1:
            return state
        pre[h] = state
        own[which, step + 1, h] = (
            factors[1] * state + factors[2] * own[which, 0, h]
            if late
            else factors[1] * own[which, step, h] + factors[2] * came
        )
        send_part(which, step + 1, h, late)
        return None

    def take_pair(which, j):
        for step in range(steps - 1):
            for late in (False, True):
                await_part(which, step, 2 * j + int(late), late)
            for late in (False, True):
                h = 2 * j + int(late)
                take(which, step, h, late, rate_ref[h])

    def finish_pairs(which, work):
        def go(j, carried):
            for late in (False, True):
                await_part(which, steps - 1, 2 * j + int(late), late)
            for late in (False, True):
                work(2 * j + int(late), late)
            return carried
        lax.fori_loop(0, heads // 2, go, 0)

    def pairs(work, first=0):
        def go(j, carried):
            for late in (False, True):
                work(2 * j + int(late), late)
            return carried
        lax.fori_loop(first, heads // 2, go, 0)

    def part(c):
        return slice(c * CHUNK, (c + 1) * CHUNK)

    start_loads((0, 1), 2, heads)
    start_loads((2, 3), 0, heads)
    small[1].wait()
    small[2].wait()
    lax.fori_loop(0, heads, spread, 0)
    pl.semaphore_wait(barrier, shards + peers - 2)
    for k in range(1, shards):
        flag_copy(k).start()

    def make_states(h, late):
        load(0, h).wait()
        load(1, h).wait()
        rate = rate_ref[h]
        out = reach_out(rate)
        state = jnp.zeros((DH, DH), F32)
        for c in range(chunks):
            weighted = (ks[h, part(c), :].astype(F32) * (out * out_mask[c])).astype(BF16)
            add = dot(weighted, vs[h, part(c), :], 0, 0)
            d_state[h, c] = add
            keep = carry(rate, c)
            state = keep[0:1, :] * state + add
        put(0, h, late, state)

    pairs(make_states)
    sq_acc[...] = jnp.zeros_like(sq_acc)
    cr_acc[...] = jnp.zeros_like(cr_acc)
    for k in range(1, shards):
        flag_copy(k).wait_recv()
    make_table()

    def attend(h):
        load(2, h).wait()
        load(3, h).wait()
        decay = jnp.exp(-rate_ref[h] * gap)
        reach = reach_in(rate_ref[h])
        def raw(c):
            return dot(qs[h, part(c), :], ks[h, part(c), :], 1, 1)

        ready = [raw(c) for c in range(min(AHEAD, chunks))]
        for c in range(chunks):
            scores = ready.pop(0)
            if c + AHEAD < chunks:
                ready.append(raw(c + AHEAD))
            w = (scores * (decay * joined[c])).astype(BF16)
            weights[h, c] = jnp.transpose(w)
            att[h, part(c), :] = dot(w, vs[h, part(c), :], 1, 0)
            near = (qs[h, part(c), :].astype(F32) * (reach * in_mask[c])).astype(BF16)
            qw[h, c] = jnp.transpose(near)
            gained[h, part(c), :] = gs[h, part(c), :].astype(F32) * gain_ref[pl.ds(h, 1), :]

    def attend_pair(j, carried):
        attend(2 * j)
        attend(2 * j + 1)
        take_pair(0, j)
        return carried

    lax.fori_loop(0, heads // 2, attend_pair, 0)

    def finish_attend(j, final):
        both = [(2 * j + int(late), late) for late in (False, True)]
        for h, late in both:
            await_part(0, steps - 1, h, late)
        states = [take(0, steps - 1, h, late, rate_ref[h]) for h, late in both]
        reaches = [reach_in(rate_ref[h]) for h, _ in both]
        for c in range(chunks):
            squares, crosses = sq_acc[part(c), :], cr_acc[part(c), :]
            for i, (h, _) in enumerate(both):
                small = states[i].astype(BF16)
                full_state[h, c] = small
                a = att[h, part(c), :] + (reaches[i] * in_mask[c]) * dot(qs[h, part(c), :], small, 1, 0)
                att[h, part(c), :] = a
                squares = squares + a * a
                crosses = crosses + gained[h, part(c), :] * a
                if c < chunks - 1:
                    states[i] = carry(rate_ref[h], c)[0:1, :] * states[i] + d_state[h, c]
            if final:
                x_buf[0, 0:1, part(c)] = jnp.sum(jnp.transpose(squares), axis=0, keepdims=True)
                x_buf[0, 1:2, part(c)] = jnp.sum(jnp.transpose(crosses), axis=0, keepdims=True)
            else:
                sq_acc[part(c), :] = squares
                cr_acc[part(c), :] = crosses

    def finish_early(j, carried):
        finish_attend(j, False)
        return carried

    lax.fori_loop(0, heads // 2 - 1, finish_early, 0)
    finish_attend(heads // 2 - 1, True)

    for k in reversed(range(1, peers)):
        swap_copy(k).start()
    sums = x_buf[0]
    for k in range(1, peers):
        swap_copy(k).wait_recv()
        sums = sums + x_buf[k]
    inverse = 1.0 / jnp.sqrt(sums[0:1, :] / total + EPSILON)
    coef = inverse * inverse * inverse * (sums[1:2, :] / total)
    inv_full[...] = jnp.transpose(jnp.broadcast_to(inverse, (DH, rows)))
    coef_full[...] = jnp.transpose(jnp.broadcast_to(coef, (DH, rows)))

    def make_grads(h, late):
        rate = rate_ref[h]
        state = jnp.zeros((DH, DH), F32)
        for c in reversed(range(chunks)):
            a, inv = att[h, part(c), :], inv_full[part(c), :]
            grad = (inv * gained[h, part(c), :] - a * coef_full[part(c), :]).astype(BF16)
            ga[h, part(c), :] = grad
            add = dot(qw[h, c], grad, 1, 0)
            d_grad[h, c] = add
            keep = carry(rate, c)
            state = keep[0:1, :] * state + add
        put(1, h, late, state)

    make_grads(0, False)
    make_grads(1, True)
    pairs(make_grads, 1)

    def inner_grads(h):
        rate = rate_ref[h]
        decay = jnp.exp(-rate * gap)
        reach = reach_in(rate)
        gain = gain_ref[pl.ds(h, 1), :]
        def raw(c):
            grad = ga[h, part(c), :]
            return dot(grad, vs[h, part(c), :], 1, 1), dot(grad, full_state[h, c], 1, 1)

        ready = [raw(c) for c in range(min(AHEAD_GRADS, chunks))]
        for c in range(chunks):
            wide, far = ready.pop(0)
            if c + AHEAD_GRADS < chunks:
                ready.append(raw(c + AHEAD_GRADS))
            n_out[part(c), cols(h)] = (att[h, part(c), :] * inv_full[part(c), :] * gain).astype(BF16)
            gvp[h, part(c), :] = dot(weights[h, c], ga[h, part(c), :], 1, 0)
            d = (wide * (decay * joined[c])).astype(BF16)
            gq = dot(d, ks[h, part(c), :], 1, 0) + (reach * in_mask[c]) * far
            gq_out[part(c), cols(h)] = gq.astype(BF16)
            gkp[h, part(c), :] = dot(d, qs[h, part(c), :], 0, 0)

    def inner_pair(j, carried):
        take_pair(1, j)
        inner_grads(2 * j)
        inner_grads(2 * j + 1)
        return carried

    lax.fori_loop(0, heads // 2, inner_pair, 0)

    def keep_last(h, late):
        last[h] = take(1, steps - 1, h, late, rate_ref[h])

    def drain(passes):
        def work(h, late):
            for which, step in passes:
                @pl.when(needs(which, late, step)[0])
                def _():
                    scan_copy(which, step, h, late).wait_send()
        pairs(work)

    drain([(0, step) for step in range(steps)] + [(1, step) for step in range(steps - 1)])
    for k in range(1, shards):
        flag_copy(k).wait_send()
    for k in range(1, peers):
        swap_copy(k).wait_send()
    finish_pairs(1, keep_last)
    drain([(1, steps - 1)])


def write_out(
    n_in, gq_in, gkp, gvp, ks, vs, d_grad, last, out_mask, clear, rate_rows,
    n_out, gq_out, gk_out, gv_out, gk, gv, sems, pair_sems,
):
    heads, rows, _ = ks.shape
    copies = [
        pltpu.make_async_copy(n_in, n_out, sems.at[0]),
        pltpu.make_async_copy(gq_in, gq_out, sems.at[1]),
    ]
    for copy in copies:
        copy.start()
    place = lax.broadcasted_iota(jnp.int32, (CHUNK, DH), 0).astype(F32)

    def pair_copies(j):
        width = gk.shape[1] // (heads // 2)
        cols = pl.ds(pl.multiple_of(j * width, width), width)
        return [
            pltpu.make_async_copy(gk.at[:, cols], gk_out.at[:, cols], pair_sems.at[0, j]),
            pltpu.make_async_copy(gv.at[:, cols], gv_out.at[:, cols], pair_sems.at[1, j]),
        ]

    def finish(h):
        cols = pl.ds(pl.multiple_of(h * DH, DH), DH)
        rate = rate_rows[h]
        out = jnp.exp(-rate[0:1, :] * (CHUNK - 1.0 - place))
        fade = jnp.exp(-rate * CHUNK)
        state = last[h]
        for c in reversed(range(rows // CHUNK)):
            part = slice(c * CHUNK, (c + 1) * CHUNK)
            small = state.astype(BF16)
            reach = out * out_mask[c]
            gk[part, cols] = (gkp[h, part, :] + reach * dot(vs[h, part, :], small, 1, 1)).astype(BF16)
            gv[part, cols] = (gvp[h, part, :] + reach * dot(ks[h, part, :], small, 1, 0)).astype(BF16)
            if c > 0:
                state = (clear[c] * fade)[0:1, :] * state + d_grad[h, c]

    def go(j, carried):
        finish(2 * j)
        finish(2 * j + 1)
        for copy in pair_copies(j):
            copy.start()
        return carried

    lax.fori_loop(0, heads // 2, go, 0)

    def drain(j, carried):
        for copy in pair_copies(j):
            copy.wait()
        return carried

    lax.fori_loop(0, heads // 2, drain, 0)
    for copy in copies:
        copy.wait()


def body(shards, peers, query_rows, key_rows, value_rows, decay_rate, starts, norm_gain, grad_out):
    rows, features = query_rows.shape
    heads = features // DH
    chunks = rows // CHUNK
    steps = (shards - 1).bit_length()
    big = jax.ShapeDtypeStruct((rows, features), BF16)
    whole = pl.BlockSpec(memory_space=pltpu.HBM)
    inside = pl.BlockSpec(memory_space=pltpu.VMEM)

    def head_rows(dtype):
        return pltpu.VMEM((heads, rows, DH), dtype)

    dma = pltpu.SemaphoreType.DMA
    handed = (
        (pltpu.VMEM((rows, features), BF16),) * 2
        + (head_rows(F32),) * 2
        + (head_rows(BF16),) * 2
        + (
            pltpu.VMEM((heads, chunks, DH, DH), F32),
            pltpu.VMEM((heads, DH, DH), F32),
            pltpu.VMEM((chunks, CHUNK, DH), F32),
            pltpu.VMEM((chunks, 8, DH), F32),
            pltpu.VMEM((heads, 8, DH), F32),
        )
    )
    kept = pl.pallas_call(
        functools.partial(kernel, shards, steps, peers, HEADS * DH),
        out_shape=handed,
        in_specs=[whole] * 7,
        out_specs=(inside,) * len(handed),
        scratch_shapes=[
            pltpu.SMEM((heads,), F32),
            pltpu.VMEM((1, rows), jnp.int32),
            pltpu.VMEM((heads, DH), F32),
        ]
        + [head_rows(BF16)] * 2
        + [pltpu.VMEM((heads, chunks, DH, CHUNK), BF16), head_rows(F32)]
        + [head_rows(F32), head_rows(BF16), pltpu.VMEM((heads, chunks, CHUNK, CHUNK), BF16)]
        + [
            pltpu.VMEM((chunks, CHUNK, CHUNK), F32),
            pltpu.VMEM((chunks, CHUNK, DH), F32),
            pltpu.VMEM((heads, chunks, DH, DH), F32),
            pltpu.VMEM((heads, chunks, DH, DH), BF16),
            pltpu.VMEM((2, steps, heads, DH, DH), F32),
            pltpu.VMEM((2, steps, heads, DH, DH), F32),
            pltpu.VMEM((heads, DH, DH), F32),
            pltpu.VMEM((shards, 8, DH), F32),
            pltpu.VMEM((12 * steps, 8, DH), F32),
            pltpu.VMEM((rows, DH), F32),
            pltpu.VMEM((rows, DH), F32),
            pltpu.VMEM((rows, DH), F32),
            pltpu.VMEM((rows, DH), F32),
            pltpu.VMEM((peers, 2, rows), F32),
            dma((3,)),
            dma((4, heads)),
            dma((2, steps, heads)),
            dma((2, steps, heads)),
            dma((shards,)),
            dma((shards,)),
            dma((peers,)),
            dma((peers,)),
        ],
        compiler_params=pltpu.CompilerParams(
            collective_id=0, has_side_effects=True, vmem_limit_bytes=34 * 1024 * 1024
        ),
    )(
        query_rows, key_rows, value_rows, grad_out, decay_rate,
        starts.reshape(1, rows), norm_gain.reshape(heads, DH),
    )
    return pl.pallas_call(
        write_out,
        out_shape=(big,) * 4,
        in_specs=[inside] * len(handed),
        out_specs=(whole,) * 4,
        scratch_shapes=[
            pltpu.VMEM((rows, features), BF16),
            pltpu.VMEM((rows, features), BF16),
            dma((2,)),
            dma((2, heads // 2)),
        ],
        compiler_params=pltpu.CompilerParams(vmem_limit_bytes=6 * 1024 * 1024),
    )(*kept)


def solution(mesh):
    both = P("ctx", "head")
    return jax.shard_map(
        functools.partial(body, mesh.shape["ctx"], mesh.shape["head"]),
        mesh=mesh,
        in_specs=(both, both, both, P("head"), P("ctx"), P("head"), both),
        out_specs=(both,) * 4,
        check_vma=False,
    )
```

```python
import functools

import jax
import jax.numpy as jnp
from jax import lax
from jax.experimental import pallas as pl
from jax.experimental.pallas import tpu as pltpu
from jax.sharding import PartitionSpec as P

HEADS = 64
DH = 128
CHUNK = 128
AHEAD = 2
AHEAD_GRADS = 3
EPSILON = 1e-06
MESH = pl.DeviceIdType.MESH
F32 = jnp.float32
BF16 = jnp.bfloat16


def dot(a, b, da, db):
    return lax.dot_general(a, b, (((da,), (db,)), ((), ())), preferred_element_type=F32)


def kernel(
    shards, steps, peers, total,
    q_hbm, k_hbm, v_hbm, g_hbm, rate_hbm, starts_hbm, gain_hbm,
    n_out, gq_out, gkp, gvp, ks, vs, d_grad, last, out_mask, clear, rate_rows,
    rate_ref, starts_ref, gain_ref,
    qs, gs, qw, gained, att, ga, weights,
    joined, in_mask, d_state, entry,
    own, got, pre, flags_buf, kept_buf, sq_acc, cr_acc, inv_full, coef_full, x_buf,
    small_sem, in_sem, s_send, s_recv, f_send, f_recv, x_send, x_recv,
):
    heads, rows, _ = qs.shape
    chunks = rows // CHUNK
    ctx = lax.axis_index("ctx")
    me = lax.axis_index("head")

    def cols(h):
        return pl.ds(pl.multiple_of(h * DH, DH), DH)

    def load(i, h):
        hbm, buf = ((k_hbm, ks), (v_hbm, vs), (q_hbm, qs), (g_hbm, gs))[i]
        return pltpu.make_async_copy(hbm.at[:, cols(h)], buf.at[h], in_sem.at[i, h])

    def size_of(late, step):
        return 1 << (steps - 1 - step if late else step)

    def scan_copy(which, step, h, late):
        size = size_of(late, step)
        return pltpu.make_async_remote_copy(
            src_ref=own.at[which, step, h],
            dst_ref=got.at[which, step, h],
            send_sem=s_send.at[which, step, h],
            recv_sem=s_recv.at[which, step, h],
            device_id=(ctx + size - 2 * size * ((ctx // size) % 2), me),
            device_id_type=MESH,
        )

    def flag_copy(k):
        return pltpu.make_async_remote_copy(
            src_ref=flags_buf.at[ctx],
            dst_ref=flags_buf.at[ctx],
            send_sem=f_send.at[k],
            recv_sem=f_recv.at[k],
            device_id=((ctx + k) % shards, me),
            device_id_type=MESH,
        )

    def across(k):
        other = me
        for bit in range(peers.bit_length()):
            size = 1 << bit
            if k & size:
                other = other + size - 2 * size * ((me // size) % 2)
        return other

    def swap_copy(k):
        return pltpu.make_async_remote_copy(
            src_ref=x_buf.at[0],
            dst_ref=x_buf.at[k],
            send_sem=x_send.at[k],
            recv_sem=x_recv.at[k],
            device_id=(ctx, across(k)),
            device_id_type=MESH,
        )

    barrier = pltpu.get_barrier_semaphore()
    for k in range(1, shards):
        pl.semaphore_signal(
            barrier, inc=1, device_id=((ctx + k) % shards, me), device_id_type=MESH
        )

    def greet(k, c):
        pl.semaphore_signal(
            barrier, inc=1, device_id=(ctx, (me + k) % peers), device_id_type=MESH
        )
        return c

    lax.fori_loop(1, peers, greet, 0)

    small = [
        pltpu.make_async_copy(hbm, inside, small_sem.at[i])
        for i, (hbm, inside) in enumerate(
            ((starts_hbm, starts_ref), (rate_hbm, rate_ref), (gain_hbm, gain_ref))
        )
    ]
    for copy in small:
        copy.start()

    def start_loads(pair, first, last):
        def go(h, c):
            for i in pair:
                load(i, h).start()
            return c
        lax.fori_loop(first, last, go, 0)

    start_loads((0, 1), 0, 2)
    small[0].wait()

    row_at = lax.broadcasted_iota(jnp.int32, (CHUNK, CHUNK), 0)
    col_at = lax.broadcasted_iota(jnp.int32, (CHUNK, CHUNK), 1)
    lower = row_at >= col_at
    ones_low = jnp.where(lower, 1.0, 0.0).astype(BF16)
    for c in range(chunks):
        flags = starts_ref[:, c * CHUNK:(c + 1) * CHUNK].astype(F32)
        wide = jnp.broadcast_to(flags, (DH, CHUNK)).astype(BF16)
        run_row = dot(wide, ones_low, 1, 1)[0:1, :]
        run_col = dot(ones_low, wide, 1, 1)
        count = jnp.sum(flags, axis=1, keepdims=True)
        both = jnp.concatenate([run_col] * (CHUNK // DH), axis=1)
        joined[c] = jnp.where(lower & (both == run_row), 1.0, 0.0)
        in_mask[c] = jnp.where(run_col == 0.0, 1.0, 0.0)
        out_mask[c] = jnp.where(run_col == count, 1.0, 0.0)
        clear[c] = jnp.broadcast_to(jnp.where(count == 0.0, 1.0, 0.0), (8, DH))
    whole = jnp.sum(starts_ref[...].astype(F32), axis=1, keepdims=True)
    flags_buf[ctx] = jnp.broadcast_to(jnp.where(whole == 0.0, 1.0, 0.0), (8, DH))

    place = lax.broadcasted_iota(jnp.int32, (CHUNK, DH), 0).astype(F32)
    gap = jnp.maximum(row_at - col_at, 0).astype(F32)

    def reach_in(rate):
        return jnp.exp(-rate * (place + 1.0))

    def reach_out(rate):
        return jnp.exp(-rate * (CHUNK - 1.0 - place))

    def carry(rate, c):
        return clear[c] * jnp.exp(jnp.full((8, DH), -rate * CHUNK, F32))

    def spread(h, c):
        rate_rows[h] = jnp.full((8, DH), rate_ref[h], F32)
        return c

    def needs(which, late, step):
        at = shards - 1 - ctx if which else ctx
        size = size_of(late, step)
        upper = (at // size) % 2 == 1
        above = at // (2 * size)
        both = (above > 0) if late else (above < shards // (2 * size) - 1)
        return ~upper | both, upper | both

    def send_part(which, step, h, late):
        @pl.when(needs(which, late, step)[0])
        def _():
            scan_copy(which, step, h, late).start()

    table = {}

    def factor(which, first, last, use, other):
        kept = jnp.ones((8, DH), F32)
        for i in range(shards):
            flag = flags_buf[shards - 1 - i if which else i]
            kept = kept * jnp.where((i >= first) & (i < last), flag, 1.0)
        slot = sum(len(entry) for entry in table.values())
        kept_buf[slot] = jnp.where(use, kept, other)
        return slot, jnp.where(use, jnp.maximum(last - first, 0) * rows, 0).astype(F32)

    def make_table():
        for which in range(2):
            at = shards - 1 - ctx if which else ctx
            for late in (False, True):
                for step in range(steps):
                    size = size_of(late, step)
                    start = at - at % (2 * size)
                    middle, end, upper = start + size, start + 2 * size, at >= start + size
                    key = (which, late, step)
                    table[key] = []
                    if not late:
                        entries = [(middle, at, upper, 0.0), (middle, end, ~upper, 1.0), (middle, end, upper, 1.0)]
                    else:
                        size = size_of(late, min(step + 1, steps - 1))
                        begin = at - at % (2 * size)
                        half = begin + size
                        lower = at < half
                        first = (at - middle + start + 1, middle, upper, 0.0) if step == 0 else (start, middle, upper, 1.0)
                        entries = [first, (begin, half, lower, 1.0), (at + 1, half, lower, 0.0)]
                    for entry in entries[:1] if step == steps - 1 else entries:
                        table[key] = table[key] + [factor(which, *entry)]

    def put(which, h, late, state):
        own[which, 0, h] = state
        send_part(which, 0, h, late)

    def await_part(which, step, h, late):
        @pl.when(needs(which, late, step)[1])
        def _():
            scan_copy(which, step, h, late).wait_recv()

    def take(which, step, h, late, rate):
        needed = needs(which, late, step)[1]
        factors = [
            (kept_buf[slot] * jnp.exp(jnp.full((8, DH), -rate * length, F32)))[0:1, :]
            for slot, length in table[which, late, step]
        ]
        came = jnp.where(needed, got[which, step, h], 0.0)
        if not late:
            state = factors[0] * came
            if step > 0:
                state = state + pre[h]
        else:
            state = factors[0] * (came if step == 0 else pre[h])
            if step > 0:
                state = state + came
        if step == steps - 1:
            return state
        pre[h] = state
        own[which, step + 1, h] = (
            factors[1] * state + factors[2] * own[which, 0, h]
            if late
            else factors[1] * own[which, step, h] + factors[2] * came
        )
        send_part(which, step + 1, h, late)
        return None

    def take_pair(which, j):
        for step in range(steps - 1):
            for late in (False, True):
                await_part(which, step, 2 * j + int(late), late)
            for late in (False, True):
                h = 2 * j + int(late)
                take(which, step, h, late, rate_ref[h])

    def finish_pairs(which, work):
        def go(j, carried):
            for late in (False, True):
                await_part(which, steps - 1, 2 * j + int(late), late)
            for late in (False, True):
                work(2 * j + int(late), late)
            return carried
        lax.fori_loop(0, heads // 2, go, 0)

    def pairs(work, first=0):
        def go(j, carried):
            for late in (False, True):
                work(2 * j + int(late), late)
            return carried
        lax.fori_loop(first, heads // 2, go, 0)

    def part(c):
        return slice(c * CHUNK, (c + 1) * CHUNK)

    start_loads((0, 1), 2, heads)
    start_loads((2, 3), 0, heads)
    small[1].wait()
    small[2].wait()
    lax.fori_loop(0, heads, spread, 0)
    pl.semaphore_wait(barrier, shards + peers - 2)
    for k in range(1, shards):
        flag_copy(k).start()

    def make_states(h, late):
        load(0, h).wait()
        load(1, h).wait()
        rate = rate_ref[h]
        out = reach_out(rate)
        state = jnp.zeros((DH, DH), F32)
        for c in range(chunks):
            weighted = (ks[h, part(c), :].astype(F32) * (out * out_mask[c])).astype(BF16)
            add = dot(weighted, vs[h, part(c), :], 0, 0)
            d_state[h, c] = add
            keep = carry(rate, c)
            state = keep[0:1, :] * state + add
        put(0, h, late, state)

    pairs(make_states)
    sq_acc[...] = jnp.zeros_like(sq_acc)
    cr_acc[...] = jnp.zeros_like(cr_acc)
    for k in range(1, shards):
        flag_copy(k).wait_recv()
    make_table()

    def attend(h):
        load(2, h).wait()
        load(3, h).wait()
        decay = jnp.exp(-rate_ref[h] * gap)
        reach = reach_in(rate_ref[h])
        def raw(c):
            return dot(qs[h, part(c), :], ks[h, part(c), :], 1, 1)

        ready = [raw(c) for c in range(min(AHEAD, chunks))]
        state = jnp.zeros((DH, DH), F32)
        for c in range(chunks):
            scores = ready.pop(0)
            if c + AHEAD < chunks:
                ready.append(raw(c + AHEAD))
            w = (scores * (decay * joined[c])).astype(BF16)
            weights[h, c] = jnp.transpose(w)
            local = dot(w, vs[h, part(c), :], 1, 0)
            if c > 0:
                local = local + (reach * in_mask[c]) * dot(qs[h, part(c), :], state.astype(BF16), 1, 0)
            att[h, part(c), :] = local
            if c < chunks - 1:
                state = carry(rate_ref[h], c)[0:1, :] * state + d_state[h, c] if c > 0 else d_state[h, c]
            near = (qs[h, part(c), :].astype(F32) * (reach * in_mask[c])).astype(BF16)
            qw[h, c] = jnp.transpose(near)
            gained[h, part(c), :] = gs[h, part(c), :].astype(F32) * gain_ref[pl.ds(h, 1), :]

    def attend_pair(j, carried):
        attend(2 * j)
        attend(2 * j + 1)
        take_pair(0, j)
        return carried

    lax.fori_loop(0, heads // 2, attend_pair, 0)

    def finish_attend(j, final):
        both = [(2 * j + int(late), late) for late in (False, True)]
        for h, late in both:
            await_part(0, steps - 1, h, late)
        states = [take(0, steps - 1, h, late, rate_ref[h]) for h, late in both]
        reaches = [reach_in(rate_ref[h]) for h, _ in both]
        for (h, _), state in zip(both, states):
            entry[h] = state
        small = [state.astype(BF16) for state in states]
        fade = [jnp.ones((1, DH), F32) for _ in both]
        for c in range(chunks):
            squares, crosses = sq_acc[part(c), :], cr_acc[part(c), :]
            for i, (h, _) in enumerate(both):
                far = (reaches[i] * fade[i]) * in_mask[c]
                a = att[h, part(c), :] + far * dot(qs[h, part(c), :], small[i], 1, 0)
                att[h, part(c), :] = a
                squares = squares + a * a
                crosses = crosses + gained[h, part(c), :] * a
                if c < chunks - 1:
                    fade[i] = carry(rate_ref[h], c)[0:1, :] * fade[i]
            if final:
                x_buf[0, 0:1, part(c)] = jnp.sum(jnp.transpose(squares), axis=0, keepdims=True)
                x_buf[0, 1:2, part(c)] = jnp.sum(jnp.transpose(crosses), axis=0, keepdims=True)
            else:
                sq_acc[part(c), :] = squares
                cr_acc[part(c), :] = crosses

    def finish_early(j, carried):
        finish_attend(j, False)
        return carried

    lax.fori_loop(0, heads // 2 - 1, finish_early, 0)
    finish_attend(heads // 2 - 1, True)

    for k in reversed(range(1, peers)):
        swap_copy(k).start()
    sums = x_buf[0]
    for k in range(1, peers):
        swap_copy(k).wait_recv()
        sums = sums + x_buf[k]
    inverse = 1.0 / jnp.sqrt(sums[0:1, :] / total + EPSILON)
    coef = inverse * inverse * inverse * (sums[1:2, :] / total)
    inv_full[...] = jnp.transpose(jnp.broadcast_to(inverse, (DH, rows)))
    coef_full[...] = jnp.transpose(jnp.broadcast_to(coef, (DH, rows)))

    def make_grads(h, late):
        rate = rate_ref[h]
        state = jnp.zeros((DH, DH), F32)
        for c in reversed(range(chunks)):
            a, inv = att[h, part(c), :], inv_full[part(c), :]
            grad = (inv * gained[h, part(c), :] - a * coef_full[part(c), :]).astype(BF16)
            ga[h, part(c), :] = grad
            add = dot(qw[h, c], grad, 1, 0)
            d_grad[h, c] = add
            keep = carry(rate, c)
            state = keep[0:1, :] * state + add
        put(1, h, late, state)

    make_grads(0, False)
    make_grads(1, True)
    pairs(make_grads, 1)

    def inner_grads(h):
        rate = rate_ref[h]
        decay = jnp.exp(-rate * gap)
        reach = reach_in(rate)
        gain = gain_ref[pl.ds(h, 1), :]
        states = [entry[h]]
        def raw(c):
            grad = ga[h, part(c), :]
            state = states.pop()
            states.append(carry(rate, c)[0:1, :] * state + d_state[h, c])
            return dot(grad, vs[h, part(c), :], 1, 1), dot(grad, state.astype(BF16), 1, 1)

        ready = [raw(c) for c in range(min(AHEAD_GRADS, chunks))]
        for c in range(chunks):
            wide, far = ready.pop(0)
            if c + AHEAD_GRADS < chunks:
                ready.append(raw(c + AHEAD_GRADS))
            n_out[part(c), cols(h)] = (att[h, part(c), :] * inv_full[part(c), :] * gain).astype(BF16)
            gvp[h, part(c), :] = dot(weights[h, c], ga[h, part(c), :], 1, 0)
            d = (wide * (decay * joined[c])).astype(BF16)
            gq = dot(d, ks[h, part(c), :], 1, 0) + (reach * in_mask[c]) * far
            gq_out[part(c), cols(h)] = gq.astype(BF16)
            gkp[h, part(c), :] = dot(d, qs[h, part(c), :], 0, 0)

    def inner_pair(j, carried):
        take_pair(1, j)
        inner_grads(2 * j)
        inner_grads(2 * j + 1)
        return carried

    lax.fori_loop(0, heads // 2, inner_pair, 0)

    def keep_last(h, late):
        last[h] = take(1, steps - 1, h, late, rate_ref[h])

    def drain(passes):
        def work(h, late):
            for which, step in passes:
                @pl.when(needs(which, late, step)[0])
                def _():
                    scan_copy(which, step, h, late).wait_send()
        pairs(work)

    drain([(0, step) for step in range(steps)] + [(1, step) for step in range(steps - 1)])
    for k in range(1, shards):
        flag_copy(k).wait_send()
    for k in range(1, peers):
        swap_copy(k).wait_send()
    finish_pairs(1, keep_last)
    drain([(1, steps - 1)])


def write_out(
    n_in, gq_in, gkp, gvp, ks, vs, d_grad, last, out_mask, clear, rate_rows,
    n_out, gq_out, gk_out, gv_out, gk, gv, sems, pair_sems,
):
    heads, rows, _ = ks.shape
    copies = [
        pltpu.make_async_copy(n_in, n_out, sems.at[0]),
        pltpu.make_async_copy(gq_in, gq_out, sems.at[1]),
    ]
    for copy in copies:
        copy.start()
    place = lax.broadcasted_iota(jnp.int32, (CHUNK, DH), 0).astype(F32)

    def pair_copies(j):
        width = gk.shape[1] // (heads // 2)
        cols = pl.ds(pl.multiple_of(j * width, width), width)
        return [
            pltpu.make_async_copy(gk.at[:, cols], gk_out.at[:, cols], pair_sems.at[0, j]),
            pltpu.make_async_copy(gv.at[:, cols], gv_out.at[:, cols], pair_sems.at[1, j]),
        ]

    def finish(h):
        cols = pl.ds(pl.multiple_of(h * DH, DH), DH)
        rate = rate_rows[h]
        out = jnp.exp(-rate[0:1, :] * (CHUNK - 1.0 - place))
        fade = jnp.exp(-rate * CHUNK)
        state = last[h]
        for c in reversed(range(rows // CHUNK)):
            part = slice(c * CHUNK, (c + 1) * CHUNK)
            small = state.astype(BF16)
            reach = out * out_mask[c]
            gk[part, cols] = (gkp[h, part, :] + reach * dot(vs[h, part, :], small, 1, 1)).astype(BF16)
            gv[part, cols] = (gvp[h, part, :] + reach * dot(ks[h, part, :], small, 1, 0)).astype(BF16)
            if c > 0:
                state = (clear[c] * fade)[0:1, :] * state + d_grad[h, c]

    def go(j, carried):
        finish(2 * j)
        finish(2 * j + 1)
        for copy in pair_copies(j):
            copy.start()
        return carried

    lax.fori_loop(0, heads // 2, go, 0)

    def drain(j, carried):
        for copy in pair_copies(j):
            copy.wait()
        return carried

    lax.fori_loop(0, heads // 2, drain, 0)
    for copy in copies:
        copy.wait()


def body(shards, peers, query_rows, key_rows, value_rows, decay_rate, starts, norm_gain, grad_out):
    rows, features = query_rows.shape
    heads = features // DH
    chunks = rows // CHUNK
    steps = (shards - 1).bit_length()
    big = jax.ShapeDtypeStruct((rows, features), BF16)
    whole = pl.BlockSpec(memory_space=pltpu.HBM)
    inside = pl.BlockSpec(memory_space=pltpu.VMEM)

    def head_rows(dtype):
        return pltpu.VMEM((heads, rows, DH), dtype)

    dma = pltpu.SemaphoreType.DMA
    handed = (
        (pltpu.VMEM((rows, features), BF16),) * 2
        + (head_rows(F32),) * 2
        + (head_rows(BF16),) * 2
        + (
            pltpu.VMEM((heads, chunks, DH, DH), F32),
            pltpu.VMEM((heads, DH, DH), F32),
            pltpu.VMEM((chunks, CHUNK, DH), F32),
            pltpu.VMEM((chunks, 8, DH), F32),
            pltpu.VMEM((heads, 8, DH), F32),
        )
    )
    kept = pl.pallas_call(
        functools.partial(kernel, shards, steps, peers, HEADS * DH),
        out_shape=handed,
        in_specs=[whole] * 7,
        out_specs=(inside,) * len(handed),
        scratch_shapes=[
            pltpu.SMEM((heads,), F32),
            pltpu.VMEM((1, rows), jnp.int32),
            pltpu.VMEM((heads, DH), F32),
        ]
        + [head_rows(BF16)] * 2
        + [pltpu.VMEM((heads, chunks, DH, CHUNK), BF16), head_rows(F32)]
        + [head_rows(F32), head_rows(BF16), pltpu.VMEM((heads, chunks, CHUNK, CHUNK), BF16)]
        + [
            pltpu.VMEM((chunks, CHUNK, CHUNK), F32),
            pltpu.VMEM((chunks, CHUNK, DH), F32),
            pltpu.VMEM((heads, chunks, DH, DH), F32),
            pltpu.VMEM((heads, DH, DH), F32),
            pltpu.VMEM((2, steps, heads, DH, DH), F32),
            pltpu.VMEM((2, steps, heads, DH, DH), F32),
            pltpu.VMEM((heads, DH, DH), F32),
            pltpu.VMEM((shards, 8, DH), F32),
            pltpu.VMEM((12 * steps, 8, DH), F32),
            pltpu.VMEM((rows, DH), F32),
            pltpu.VMEM((rows, DH), F32),
            pltpu.VMEM((rows, DH), F32),
            pltpu.VMEM((rows, DH), F32),
            pltpu.VMEM((peers, 2, rows), F32),
            dma((3,)),
            dma((4, heads)),
            dma((2, steps, heads)),
            dma((2, steps, heads)),
            dma((shards,)),
            dma((shards,)),
            dma((peers,)),
            dma((peers,)),
        ],
        compiler_params=pltpu.CompilerParams(
            collective_id=0, has_side_effects=True, vmem_limit_bytes=34 * 1024 * 1024
        ),
    )(
        query_rows, key_rows, value_rows, grad_out, decay_rate,
        starts.reshape(1, rows), norm_gain.reshape(heads, DH),
    )
    return pl.pallas_call(
        write_out,
        out_shape=(big,) * 4,
        in_specs=[inside] * len(handed),
        out_specs=(whole,) * 4,
        scratch_shapes=[
            pltpu.VMEM((rows, features), BF16),
            pltpu.VMEM((rows, features), BF16),
            dma((2,)),
            dma((2, heads // 2)),
        ],
        compiler_params=pltpu.CompilerParams(vmem_limit_bytes=6 * 1024 * 1024),
    )(*kept)


def solution(mesh):
    both = P("ctx", "head")
    return jax.shard_map(
        functools.partial(body, mesh.shape["ctx"], mesh.shape["head"]),
        mesh=mesh,
        in_specs=(both, both, both, P("head"), P("ctx"), P("head"), both),
        out_specs=(both,) * 4,
        check_vma=False,
    )
```
